32 devices in a mesh: grp: 8 (over z, core), dev: 4 (over y, x).
Axes of the slice: x: 2, y: 2, z: 4, core: 2. Of those that a mesh axis runs over, the one named last changes fastest.
Arguments:
- tokens: bfloat16 [4096, 2304], P(('grp', 'dev')), may hold values from -6 to 6
- cotangent: bfloat16 [4096, 2304], P(('grp', 'dev')), may hold values from -6 to 6
- expert_ids: int32 [4096, 8], P(('grp', 'dev')), may hold values from 0 to 31, as said below
- combine_weights: bfloat16 [4096, 8], P(('grp', 'dev')), may hold values from 0.099609375 to 0.3984375
- live_counts: int32 [32, 2], P(('grp', 'dev')), may hold values from 32 to 64, as said below
- gate_weight: bfloat16 [32, 2304, 512], P(('grp', 'dev')), may hold values from -0.125 to 0.125
- up_weight: bfloat16 [32, 2304, 512], P(('grp', 'dev')), may hold values from -0.125 to 0.125
- down_weight: bfloat16 [32, 512, 2304], P(('grp', 'dev')), may hold values from -0.25 to 0.25
Outputs:
- mixed_out: bfloat16 [4096, 2304], P(('grp', 'dev'))
- input_grad: bfloat16 [4096, 2304], P(('grp', 'dev'))
The draws below stay inside these ranges and needn't reach their ends.
Inputs may be any that keep to these rules, and one draw needn't show every extreme that they name: `expert_ids`: expert g * 4 + l is expert l of group g. Each row names 8 distinct experts lying in 4 distinct groups, 2 in each, and entries 2 q to 2 q + 1 share one group. Counting all 64 rows of one device's micro-batch, live or not, each expert is named by exactly 16 rows and each group by exactly 32 rows; so at most 16 live rows name one expert, exactly 16 in a full micro-batch. The first live_counts[d, m] rows of device d's micro-batch m are live, the others are padding; some micro-batch of some device is full.
All inputs are finite; a program needn't handle non-finite values.
Results may differ from the reference program's by a relative error of at most 0.0085.
Values may be sent and summed in bfloat16 or wider, within the bound.
A program may use at most 128 MiB of HBM per device.

```python
import jax
import jax.numpy as jnp
from jax import lax

D = 2304
F = 512
TOPK = 8
TOPG = 4
PAIR = 2
MICRO = 2
MB_ROWS = 64
TOK_DEV = 128
GROUPS = 8
GROUP_SIZE = 4
EXPERTS = 32
TOKENS = 4096
CAP = 16
DEVICES = 32


def draw_expert_ids(key, part):
    per_group = MB_ROWS // GROUPS
    stride = GROUPS // TOPG
    base_key = jax.random.fold_in(key, 301)

    def one_block(index):
        block_key = jax.random.fold_in(base_key, index)
        group_perm = jax.random.permutation(jax.random.fold_in(block_key, 1), GROUPS).astype(jnp.int32)
        local_keys = jax.random.split(jax.random.fold_in(block_key, 2), GROUPS)
        local_perm = jax.vmap(lambda one_key: jax.random.permutation(one_key, GROUP_SIZE))(local_keys).astype(jnp.int32)
        row_perm = jax.random.permutation(jax.random.fold_in(block_key, 3), MB_ROWS).astype(jnp.int32)
        quarter = jnp.arange(TOPG, dtype=jnp.int32)
        order_scores = jax.random.randint(jax.random.fold_in(block_key, 4), (MB_ROWS, TOPG), 0, 1024, dtype=jnp.int32) * TOPG + quarter[None, :]
        slot_order = jnp.argsort(order_scores, axis=1).astype(jnp.int32)
        base_rows = jnp.arange(MB_ROWS, dtype=jnp.int32)
        row_class = base_rows % GROUPS
        row_above = base_rows // GROUPS
        group_raw = (row_class[:, None] + quarter[None, :] * stride) % GROUPS
        within = quarter[None, :] * per_group + row_above[:, None]
        pair_range = jnp.arange(PAIR, dtype=jnp.int32)
        local_raw = (within[:, :, None] + pair_range[None, None, :] * (GROUP_SIZE // PAIR)) % GROUP_SIZE
        group_ids = group_perm[group_raw]
        local_ids = local_perm[group_raw[:, :, None], local_raw]
        full_ids = group_ids[:, :, None] * GROUP_SIZE + local_ids
        full_ids = jnp.take_along_axis(full_ids, slot_order[:, :, None], axis=1)
        full_ids = full_ids[row_perm]
        return full_ids.reshape(MB_ROWS, TOPK).astype(jnp.int32)
    blocks = jax.vmap(one_block)(jnp.arange(DEVICES * MICRO, dtype=jnp.int32))
    return blocks.reshape(DEVICES * MICRO * MB_ROWS, TOPK).astype(jnp.int32)


def draw_live_counts(key, part):
    entries = DEVICES * MICRO
    base_counts = jax.random.randint(jax.random.fold_in(key, 201), (DEVICES, MICRO), MB_ROWS // 2, MB_ROWS + 1, dtype=jnp.int32)
    full_entry = jax.random.randint(jax.random.fold_in(key, 202), (), 0, entries, dtype=jnp.int32)
    low_step = jax.random.randint(jax.random.fold_in(key, 203), (), 0, entries - 1, dtype=jnp.int32)
    low_entry = (full_entry + 1 + low_step) % entries
    flat_entry = jnp.arange(entries, dtype=jnp.int32).reshape(DEVICES, MICRO)
    counts = jnp.where(flat_entry == low_entry, MB_ROWS // 2, base_counts)
    return jnp.where(flat_entry == full_entry, MB_ROWS, counts).astype(jnp.int32)


def steps_of(own_key, shape, cuts, low, high):
    def one(dim, parts):
        steps = jax.random.uniform(jax.random.fold_in(jax.random.fold_in(own_key, 6), dim), (parts,), jnp.float32, low / len(cuts), high / len(cuts))
        return jnp.repeat(jnp.exp(steps), shape[dim] // parts).reshape((-1,) + (1,) * (len(shape) - dim - 1))

    gain = one(*cuts[0])
    for cut in cuts[1:]:
        gain = gain * one(*cut)
    return gain


def bell_draw(stream_key, shape, deviation, most, cuts=(), held_as=jnp.bfloat16):
    result = jax.random.normal(stream_key, shape, jnp.float32) * deviation
    if len(cuts) > 0:
        result = steps_of(stream_key, shape, cuts, -0.22, 0.18) * result
    return jnp.clip(result, min=-most, max=most).astype(held_as)


def setup_inputs(seed: int = 0) -> dict:
    seeds = jax.random.split(jax.random.key(seed), 9)
    tokens = bell_draw(seeds[0], (TOKENS, D), 1.0, 6.0, ((0, 32),))
    cotangent = bell_draw(seeds[1], (TOKENS, D), 1.0, 6.0, ((0, 32),))
    expert_ids = draw_expert_ids(jax.random.fold_in(seeds[8], 71), 0)
    combine_weights = jnp.clip(0.099609375 + 0.29882812 * jax.random.uniform(seeds[3], (TOKENS, TOPK), jnp.float32) ** steps_of(seeds[3], (TOKENS, TOPK), ((0, 32),), -0.2, 0.2), 0.099609375, 0.3984375).astype(jnp.bfloat16)
    live_counts = draw_live_counts(jax.random.fold_in(seeds[8], 71), 0)
    gate_weight = bell_draw(seeds[5], (EXPERTS, D, F), D ** -0.5, 0.125, ((0, 32),))
    up_weight = bell_draw(seeds[6], (EXPERTS, D, F), D ** -0.5, 0.125, ((0, 32),))
    down_weight = bell_draw(seeds[7], (EXPERTS, F, D), F ** -0.5, 0.25, ((0, 32),))
    return {"tokens": tokens, "cotangent": cotangent, "expert_ids": expert_ids, "combine_weights": combine_weights, "live_counts": live_counts, "gate_weight": gate_weight, "up_weight": up_weight, "down_weight": down_weight}


def expert_pass(rows_x, rows_dy, gate_matrix, up_matrix, down_matrix):
    contract = (((1,), (1,)), ((), ()))
    gate_pre = jnp.dot(rows_x, gate_matrix, preferred_element_type=jnp.float32)
    up_pre = jnp.dot(rows_x, up_matrix, preferred_element_type=jnp.float32)
    sigmoid_gate = jax.nn.sigmoid(gate_pre)
    gate_act = gate_pre * sigmoid_gate
    hidden = (gate_act * up_pre).astype(jnp.bfloat16)
    out_rows = jnp.dot(hidden, down_matrix, preferred_element_type=jnp.float32).astype(jnp.bfloat16)
    hidden_grad = lax.dot_general(rows_dy, down_matrix, contract, preferred_element_type=jnp.float32)
    gate_grad = (hidden_grad * up_pre * sigmoid_gate * (1.0 + gate_pre * (1.0 - sigmoid_gate))).astype(jnp.bfloat16)
    up_grad = (hidden_grad * gate_act).astype(jnp.bfloat16)
    grad_rows = lax.dot_general(gate_grad, gate_matrix, contract, preferred_element_type=jnp.float32)
    grad_rows = grad_rows + lax.dot_general(up_grad, up_matrix, contract, preferred_element_type=jnp.float32)
    return out_rows, grad_rows.astype(jnp.bfloat16)


def combine_device(pieces):
    store_piece, weight_piece = pieces
    pair_rows = store_piece.astype(jnp.float32)
    scaled = jnp.sum(weight_piece[..., None] * pair_rows, axis=2).astype(jnp.bfloat16)
    return jnp.sum(scaled.astype(jnp.float32), axis=1).astype(jnp.bfloat16)


def reference(tokens, cotangent, expert_ids, combine_weights, live_counts, gate_weight, up_weight, down_weight):
    expert_range = jnp.arange(EXPERTS, dtype=jnp.int32)
    picked = expert_ids.reshape(DEVICES, MICRO, MB_ROWS, TOPK)
    position = jnp.arange(MB_ROWS, dtype=jnp.int32)
    alive_rows = position[None, None, :] < live_counts[:, :, None]
    alive_int = alive_rows.astype(jnp.int32)
    member = jnp.sum((picked[..., None] == expert_range).astype(jnp.int32), axis=3) * alive_int[..., None]
    earlier = jnp.cumsum(member, axis=2) - member
    slot_index = jnp.take_along_axis(earlier, picked, axis=3)
    device_index = jnp.arange(DEVICES, dtype=jnp.int32)[:, None, None, None]
    micro_index = jnp.arange(MICRO, dtype=jnp.int32)[None, :, None, None]
    per_expert = DEVICES * MICRO * CAP
    flat_slot = ((picked * DEVICES + device_index) * MICRO + micro_index) * CAP + slot_index
    flat_slot = jnp.where(alive_rows[..., None], flat_slot, EXPERTS * per_expert).astype(jnp.int32)
    assign_count = TOKENS * TOPK
    owner = jnp.full((EXPERTS * per_expert,), assign_count, dtype=jnp.int32)
    owner = owner.at[flat_slot.reshape(-1)].set(jnp.arange(assign_count, dtype=jnp.int32), mode="drop")
    owner = owner.reshape(EXPERTS, per_expert)
    zero_row = jnp.zeros((1, D), tokens.dtype)
    padded_tokens = jnp.concatenate([tokens, zero_row], axis=0)
    padded_cotan = jnp.concatenate([cotangent, zero_row], axis=0)

    def visit_expert(carried, inputs):
        out_store, grad_store = carried
        owner_rows, gate_matrix, up_matrix, down_matrix = inputs
        token_rows = owner_rows // TOPK
        expert_out, expert_grad = expert_pass(padded_tokens[token_rows], padded_cotan[token_rows], gate_matrix, up_matrix, down_matrix)
        return (out_store.at[owner_rows].set(expert_out), grad_store.at[owner_rows].set(expert_grad)), None

    empty_store = jnp.zeros((assign_count + 1, D), tokens.dtype)
    stores = lax.scan(visit_expert, (empty_store, empty_store), (owner, gate_weight, up_weight, down_weight))[0]
    live_weights = combine_weights.astype(jnp.float32) * alive_rows.reshape(TOKENS)[:, None].astype(jnp.float32)
    weight_blocks = live_weights.reshape(DEVICES, TOK_DEV, TOPG, PAIR)
    out_blocks = stores[0][:assign_count].reshape(DEVICES, TOK_DEV, TOPG, PAIR, D)
    grad_blocks = stores[1][:assign_count].reshape(DEVICES, TOK_DEV, TOPG, PAIR, D)
    mixed_out = lax.map(combine_device, (out_blocks, weight_blocks)).reshape(TOKENS, D)
    input_grad = lax.map(combine_device, (grad_blocks, weight_blocks)).reshape(TOKENS, D)
    return mixed_out, input_grad
```

```python
import functools

import jax
import jax.numpy as jnp
from jax import lax
from jax.experimental import pallas as pl
from jax.experimental.pallas import tpu as pltpu
from jax.sharding import PartitionSpec as P

PAIR = 2
LAG_EXPERT = 1
LAG_RETURN = 2
MESH = pl.DeviceIdType.MESH
TRANS_RHS = (((1,), (1,)), ((), ()))


def xor(a, b, size):
    out = 0
    bit = 1
    while bit < size:
        out = out + ((a // bit + b // bit) % 2) * bit
        bit *= 2
    return out


def chunk_order(groups):
    if groups < 8:
        return list(range(groups))
    return [0, 4, 2] + list(range(5, groups)) + [3, 1]


def distance_of(unit, parts, groups):
    i = unit // parts
    out = 0
    for k, value in enumerate(chunk_order(groups)):
        out = out + value * ((i + groups - k) // groups - (i + groups - k - 1) // groups)
    return out


def moe_kernel(
    groups,
    peers,
    joined,
    parts,
    tok_ref,
    cot_ref,
    pick_ref,
    slot_ref,
    sum_ref,
    gate_hbm,
    up_hbm,
    down_hbm,
    out_ref,
    grad_ref,
    gate_ref,
    up_ref,
    down_ref,
    zsend,
    zrecv,
    zback,
    xysend,
    xyrecv,
    xyback,
    w_sem,
    zs_sem,
    zr_sem,
    bs_sem,
    br_sem,
    ds_sem,
    dr_sem,
    rs_sem,
    rr_sem,
):
    g = lax.axis_index("grp")
    l = lax.axis_index("dev")
    width = tok_ref.shape[1]
    wide = 2 * width
    units = groups * parts
    chunks = units // joined
    group_rows = zrecv.shape[1]
    slots = slot_ref.shape[2]
    peer_rows = slots // peers

    barrier = pltpu.get_barrier_semaphore()
    for k in range(1, groups):
        pl.semaphore_signal(
            barrier, inc=1, device_id={"grp": xor(g, k, groups)}, device_id_type=MESH
        )
    for q in range(1, peers):
        pl.semaphore_signal(
            barrier, inc=1, device_id={"dev": xor(l, q, peers)}, device_id_type=MESH
        )

    loads = [
        pltpu.make_async_copy(src, dst, w_sem.at[n])
        for n, (src, dst) in enumerate(
            ((gate_hbm, gate_ref), (up_hbm, up_ref), (down_hbm, down_ref))
        )
    ]
    for load in loads:
        load.start()

    def z_copy(i):
        return pltpu.make_async_remote_copy(
            src_ref=zsend.at[i],
            dst_ref=zrecv.at[i],
            send_sem=zs_sem.at[i],
            recv_sem=zr_sem.at[i],
            device_id={"grp": xor(g, distance_of(i, parts, groups), groups)},
            device_id_type=MESH,
        )

    def z_back(i):
        return pltpu.make_async_remote_copy(
            src_ref=zrecv.at[i, :, pl.ds(0, wide)],
            dst_ref=zback.at[i],
            send_sem=bs_sem.at[i],
            recv_sem=br_sem.at[i],
            device_id={"grp": xor(g, distance_of(i, parts, groups), groups)},
            device_id_type=MESH,
        )

    def xy_copy(c, q):
        return pltpu.make_async_remote_copy(
            src_ref=xysend.at[c, q],
            dst_ref=xyrecv.at[c, q],
            send_sem=ds_sem.at[c, q],
            recv_sem=dr_sem.at[c, q],
            device_id={"dev": xor(l, q, peers)},
            device_id_type=MESH,
        )

    def xy_back(c, q):
        return pltpu.make_async_remote_copy(
            src_ref=xyrecv.at[c, q],
            dst_ref=xyback.at[c, q],
            send_sem=rs_sem.at[c, q],
            recv_sem=rr_sem.at[c, q],
            device_id={"dev": xor(l, q, peers)},
            device_id_type=MESH,
        )

    def fill(i, target):
        pick = pick_ref[i]
        for source, low in ((tok_ref, 0), (cot_ref, width)):
            target[i, :, low : low + width] = jnp.dot(
                pick, source[...], preferred_element_type=jnp.float32
            ).astype(jnp.bfloat16)
        target[i, :, wide : wide + slots] = jnp.dot(
            pick, slot_ref[i // parts], preferred_element_type=jnp.float32
        ).astype(jnp.bfloat16)

    for i in range(parts):
        fill(i, zrecv)

    def chunk_weights(c):
        block = zrecv[pl.ds(c * joined, joined), :, wide : wide + slots]
        return block.reshape(joined * group_rows, slots)

    def place(c):
        for j in range(joined):
            i = c * joined + j

            @pl.when(i >= parts)
            def _(i=i):
                z_copy(i).wait_recv()

        weights = chunk_weights(c).astype(jnp.float32)
        select = jnp.where(weights != 0.0, 1.0, 0.0).T.astype(jnp.bfloat16)
        rows = zrecv[pl.ds(c * joined, joined), :, 0:wide].reshape(joined * group_rows, wide)
        placed = jnp.dot(select, rows, preferred_element_type=jnp.float32).astype(jnp.bfloat16)
        for q in range(1, peers):
            xysend[c, q] = placed[q * peer_rows : (q + 1) * peer_rows]
            xy_copy(c, q).start()
        xyrecv[c, 0] = placed[0:peer_rows]

    def expert(c):
        @pl.when(c == 0)
        def _():
            for load in loads:
                load.wait()

        for q in range(1, peers):
            xy_copy(c, q).wait_recv()
        rows_x = xyrecv[c, :, :, 0:width].reshape(slots, width)
        rows_dy = xyrecv[c, :, :, width:wide].reshape(slots, width)
        gate_pre = jnp.dot(rows_x, gate_ref[...], preferred_element_type=jnp.float32)
        up_pre = jnp.dot(rows_x, up_ref[...], preferred_element_type=jnp.float32)
        act_grad = lax.dot_general(
            rows_dy, down_ref[...], TRANS_RHS, preferred_element_type=jnp.float32
        )
        sig = jax.nn.sigmoid(gate_pre)
        gate_act = gate_pre * sig
        act = (gate_act * up_pre).astype(jnp.bfloat16)
        gate_grad = (act_grad * up_pre * sig * (1.0 + gate_pre * (1.0 - sig))).astype(jnp.bfloat16)
        up_grad = (act_grad * gate_act).astype(jnp.bfloat16)
        expert_out = jnp.dot(act, down_ref[...], preferred_element_type=jnp.float32)
        xyrecv[c, :, :, 0:width] = expert_out.astype(jnp.bfloat16).reshape(peers, peer_rows, width)
        expert_grad = lax.dot_general(
            gate_grad, gate_ref[...], TRANS_RHS, preferred_element_type=jnp.float32
        ) + lax.dot_general(up_grad, up_ref[...], TRANS_RHS, preferred_element_type=jnp.float32)
        xyrecv[c, :, :, width:wide] = expert_grad.astype(jnp.bfloat16).reshape(
            peers, peer_rows, width
        )
        for q in range(1, peers):
            xy_back(c, q).start()
        xyback[c, 0] = xyrecv[c, 0]

    def combine(c):
        for q in range(1, peers):
            xy_back(c, q).wait_recv()
        weights = chunk_weights(c)
        pairs = jnp.dot(
            weights, xyback[c].reshape(slots, wide), preferred_element_type=jnp.float32
        ).astype(jnp.bfloat16)
        zrecv[pl.ds(c * joined, joined), :, 0:wide] = pairs.reshape(joined, group_rows, wide)
        for j in range(joined):
            i = c * joined + j

            @pl.when(i >= parts)
            def _():
                z_back(i).start()

    early = min(1, parts // joined)
    pl.semaphore_wait(barrier, groups + peers - 2)
    for c in range(early):
        place(c)
    fill(parts, zsend)

    def send_step(i, carry):
        fill(i, zsend)
        z_copy(i - 1).start()
        return carry

    lax.fori_loop(parts + 1, units, send_step, 0)
    z_copy(units - 1).start()

    def step(t, carry):
        @pl.when((t >= early) & (t < chunks))
        def _():
            place(t)

        @pl.when((t >= LAG_EXPERT) & (t < chunks + LAG_EXPERT))
        def _():
            expert(t - LAG_EXPERT)

        @pl.when(t >= LAG_RETURN)
        def _():
            combine(t - LAG_RETURN)

        return carry

    lax.fori_loop(0, chunks + LAG_RETURN, step, 0)

    for i in range(parts):
        zback[i] = zrecv[i, :, 0:wide]

    def finish_step(i, carry):
        z_back(i).wait_recv()
        return carry

    lax.fori_loop(parts, units, finish_step, 0)
    for target, low in ((out_ref, 0), (grad_ref, width)):
        target[...] = jnp.dot(
            sum_ref[...],
            zback[:, :, low : low + width].reshape(units * group_rows, width),
            preferred_element_type=jnp.float32,
        ).astype(jnp.bfloat16)

    def drain_z(i, carry):
        z_copy(i).wait_send()
        z_back(i).wait_send()
        return carry

    lax.fori_loop(parts, units, drain_z, 0)

    def drain_xy(c, carry):
        for q in range(1, peers):
            xy_copy(c, q).wait_send()
            xy_back(c, q).wait_send()
        return carry

    lax.fori_loop(0, chunks, drain_xy, 0)


def routing(expert_ids, combine_weights, live_counts, groups, peers, joined):
    rows, top_count = expert_ids.shape
    parts = live_counts.shape[1]
    rows_mb = rows // parts
    experts = groups * peers
    units = groups * parts
    per_expert = rows_mb * top_count // experts
    per_group = per_expert * peers // PAIR
    g = lax.axis_index("grp")
    l = lax.axis_index("dev")
    relative = ((expert_ids // peers) ^ g) * peers + ((expert_ids % peers) ^ l)
    order = jnp.array(chunk_order(groups), jnp.int32)
    wanted = (order[:, None] * peers + jnp.arange(peers, dtype=jnp.int32)).reshape(-1)
    hit = relative[:, :, None] == wanted
    member = jnp.any(hit, axis=1)
    weight = jnp.sum(
        jnp.where(hit, combine_weights.astype(jnp.float32)[:, :, None], 0.0), axis=1
    )
    index = jnp.arange(rows, dtype=jnp.int32)
    part = index // rows_mb
    live = (index % rows_mb) < jnp.repeat(live_counts[0], rows_mb)
    weight = jnp.where(live[:, None], weight, 0.0).astype(jnp.bfloat16)
    in_group = jnp.any(member.reshape(rows, groups, peers), axis=2)
    both = jnp.concatenate([member, in_group], axis=1).astype(jnp.bfloat16)
    before = (
        (index[:, None] > index[None, :]) & (part[:, None] == part[None, :])
    ).astype(jnp.bfloat16)
    rank = jnp.dot(before, both, preferred_element_type=jnp.float32).astype(jnp.int32)
    expert_rank, group_rank = rank[:, :experts], rank[:, experts:]
    group_slot = jnp.where(in_group, group_rank + part[:, None] * per_group, -1)
    unit_rows = jnp.arange(parts * per_group, dtype=jnp.int32)
    pick = (
        (group_slot.T[:, None, :] == unit_rows[None, :, None])
        .astype(jnp.bfloat16)
        .reshape(units, per_group, rows)
    )
    total = (
        (group_slot[:, :, None] == unit_rows)
        .astype(jnp.bfloat16)
        .reshape(rows, units * per_group)
    )
    width = joined * per_expert
    offset = jnp.arange(groups, dtype=jnp.int32)[None, :] * parts + part[:, None]
    expert_slot = expert_rank.reshape(rows, groups, peers) + (
        offset % joined * per_expert
    )[..., None]
    expert_slot = expert_slot.transpose(1, 0, 2)[..., None]
    slot = jnp.where(
        expert_slot == jnp.arange(width, dtype=jnp.int32),
        weight.reshape(rows, groups, peers).transpose(1, 0, 2)[..., None],
        jnp.zeros((), jnp.bfloat16),
    ).reshape(groups, rows, peers * width)
    return pick, slot, total


def general_local(
    tokens, cotangent, expert_ids, combine_weights, live_counts, gate_weight, up_weight, down_weight
):
    groups = lax.axis_size("grp")
    peers = lax.axis_size("dev")
    rows, width = tokens.shape
    hidden = gate_weight.shape[2]
    parts = live_counts.shape[1]
    units = groups * parts
    per_expert = rows // parts * expert_ids.shape[1] // (groups * peers)
    per_group = per_expert * peers // PAIR
    joined = max(1, 16 // per_expert)
    chunks = units // joined
    peer_rows = joined * per_expert
    slots = peers * peer_rows
    wide = 2 * width
    pick, slot, total = routing(
        expert_ids, combine_weights, live_counts, groups, peers, joined
    )
    vmem = pl.BlockSpec(memory_space=pltpu.VMEM)
    anywhere = pl.BlockSpec(memory_space=pl.ANY)
    dma = pltpu.SemaphoreType.DMA
    bf16 = jnp.bfloat16
    return pl.pallas_call(
        functools.partial(moe_kernel, groups, peers, joined, parts),
        out_shape=(
            jax.ShapeDtypeStruct((rows, width), bf16),
            jax.ShapeDtypeStruct((rows, width), bf16),
        ),
        in_specs=[vmem] * 5 + [anywhere] * 3,
        out_specs=(vmem, vmem),
        scratch_shapes=[
            pltpu.VMEM((width, hidden), bf16),
            pltpu.VMEM((width, hidden), bf16),
            pltpu.VMEM((hidden, width), bf16),
            pltpu.VMEM((units, per_group, wide + slots), bf16),
            pltpu.VMEM((units, per_group, wide + slots), bf16),
            pltpu.VMEM((units, per_group, wide), bf16),
            pltpu.VMEM((chunks, peers, peer_rows, wide), bf16),
            pltpu.VMEM((chunks, peers, peer_rows, wide), bf16),
            pltpu.VMEM((chunks, peers, peer_rows, wide), bf16),
            dma((3,)),
            dma((units,)),
            dma((units,)),
            dma((units,)),
            dma((units,)),
            dma((chunks, peers)),
            dma((chunks, peers)),
            dma((chunks, peers)),
            dma((chunks, peers)),
        ],
        compiler_params=pltpu.CompilerParams(
            collective_id=0, has_side_effects=True, vmem_limit_bytes=65 * 1024 * 1000
        ),
    )(
        tokens,
        cotangent,
        pick,
        slot,
        total,
        gate_weight[0],
        up_weight[0],
        down_weight[0],
    )


LANES = 128


PIECES = ((0, 0), (1, 0), (1, 1))
ARRIVE, SELECT, EXPERT, COMBINE, PAIR_SUM, REDUCE = 0, 3, 5, 6, 8, 10
OWN, PASS_OWN, FINAL, FINISH, IDLE = 13, 16, 17, 18, 19
KINDS = 32
PACKED = 3
PLAN_PARTS = 2
PLAN_4 = (
    (
        113, 129, 105, 120, 121, 2, 32, 24, 10, 18, 26, 34, 4, 40, 20, 42, 12, 28, 36, 50, 58,
        6, 7, 44, 22, 14, 38, 30, 60, 15, 52, 23, 39, 31, 46, 68, 74, 3, 76, 47, 66, 62, 5, 54,
        63, 19, 11, 55, 35, 27, 70, 71, 79, 21, 78, 13, 29, 37, 43, 45, 33, 51, 25, 61, 56, 53,
        41, 77, 69, 48, 59, 136, 57, 49, 64, 67, 75, 137, 73, 72, 144, 65, 145,
    ),
    (
        122, 131, 34, 26, 4, 1, 20, 12, 0, 28, 36, 7, 16, 6, 8, 22, 24, 32, 9, 17, 44, 14, 15,
        30, 38, 52, 33, 23, 31, 39, 107, 46, 25, 68, 5, 123, 40, 115, 60, 21, 47, 54, 13, 29,
        62, 100, 76, 37, 48, 84, 41, 63, 94, 56, 78, 27, 102, 55, 95, 35, 45, 88, 103, 57, 71,
        79, 70, 92, 49, 64, 42, 89, 96, 97, 86, 43, 72, 73, 87, 61, 53, 65, 58, 80, 93, 59, 50,
        101, 138, 51, 81, 77, 69, 85, 139, 66, 74, 67, 75, 146, 147,
    ),
)
PLANS = {4: PLAN_4}


def plan_words(depth, parts):
    count = depth * parts
    base = KINDS * count
    orders = []
    for z in range(depth):
        codes = list(PLANS[depth][min(z, depth - 1 - z)])
        if 2 * z >= depth:
            codes = [
                kind - kind % count + (depth - 1 - kind % count // parts) * parts + kind % parts
                for kind in codes
            ]
        orders.append(codes)
    length = max(len(codes) for codes in orders)
    length += -length % PACKED
    words = []
    for codes in orders:
        codes = codes + [IDLE * count] * (length - len(codes))
        words.append(
            [
                sum(codes[b + n] * base**n for n in range(PACKED))
                for b in range(0, length, PACKED)
            ]
        )
    return words


def plane_kernel(
    groups,
    parts,
    experts,
    per,
    cut,
    tok_hbm,
    cot_hbm,
    ids_ref,
    mix_ref,
    live_ref,
    gate_hbm,
    up_hbm,
    down_hbm,
    out_ref,
    grad_ref,
    gate_ref,
    up_ref,
    down_ref,
    dense_a,
    dense_b,
    hot_ref,
    slot_ref,
    weight_ref,
    send_ref,
    moved_x,
    moved_dy,
    back_ref,
    land_a,
    land_b,
    sum_a,
    sum_b,
    w_sem,
    in_sem,
    agr_sem,
    agz_sem,
    agd_sem,
    agp_sem,
    ss_sem,
    sr_sem,
    bs_sem,
    br_sem,
    ps_sem,
    pr_sem,
    ra_sem,
    rb_sem,
    rs_sem,
    fs_sem,
    fr_sem,
):
    g = lax.axis_index("grp")
    l = lax.axis_index("dev")
    depth = groups // 2
    z = g // 2
    core = g % 2
    peers = experts // groups
    rows_mb = dense_a.shape[4]
    rows = rows_mb * parts
    width = down_ref.shape[1]
    rest = width - cut
    count = depth * parts
    pair = 2 * per
    blocks = rows_mb // per
    slots = 4 * pair
    both = 2 * rows_mb
    f32 = jnp.float32
    bf16 = jnp.bfloat16
    inner = (z > 0) & (z < depth - 1)
    outer = (z == 0) | (z == depth - 1)
    dense = (dense_a, dense_b)
    size = (cut, rest)
    outs = (out_ref, grad_ref)

    flips = (l + 2 - 4 * (l // 2), l + 1 - 2 * (l % 2))

    def near(h):
        return {"grp": g, "dev": flips[1 - h]}

    def peer(h, q):
        return {
            "grp": g + (q // 2) * (1 - 2 * core),
            "dev": flips[h] if q % 2 else l,
        }

    def remote(src, dst, send, recv, device):
        return pltpu.make_async_remote_copy(
            src_ref=src,
            dst_ref=dst,
            send_sem=send,
            recv_sem=recv,
            device_id=device,
            device_id_type=MESH,
        )

    def spread_z(h, k, p, s, m, d, second=False):
        slot = dense[k].at[h, p, s, m]
        send = agd_sem.at[2 * h + k, p, m] if second else agz_sem.at[2 * h + k, p, s, m]
        return remote(
            slot, slot, send, agr_sem.at[2 * h + k, p, s, m], {"grp": g + 2 * d, "dev": l}
        )

    def spread_p(h, k, s, m):
        return remote(
            dense[k].at[h, 0, s, m],
            dense[k].at[h, 1, s, m],
            agp_sem.at[2 * h + k, s, m],
            agr_sem.at[2 * h + k, 1, s, m],
            near(h),
        )

    def moved(h, t, q):
        if h == 0:
            return moved_x.at[t, q // 2, q % 2]
        return moved_dy.at[t, q // 2, :, q % 2]

    def select_copy(h, t, q):
        return remote(
            send_ref.at[h, t, pl.ds(2 * q, 2)],
            moved(h, t, q),
            ss_sem.at[h, t, q],
            sr_sem.at[h, t, q],
            peer(h, q),
        )

    def back_copy(h, t, q):
        return remote(
            moved(h, t, q),
            back_ref.at[h, t, q],
            bs_sem.at[h, t, q],
            br_sem.at[h, t, q],
            peer(h, q),
        )

    def sums(h, k, p, t):
        low = 0 if k == 0 else cut
        return send_ref.at[h, t, pl.ds(p * blocks, blocks), :, pl.ds(low, size[k])]

    def pair_copy(h, t):
        return remote(
            sums(h, 0, 1, t), land_a.at[h, t], ps_sem.at[h, t], pr_sem.at[h, t], near(h)
        )

    def away(s):
        return jnp.where(s > z, 1, -1)

    def onward(h, k, p, s, m, src):
        slot = jnp.where(s == z + 1, depth, s)
        if k == 0:
            dst, recv = sum_a.at[h, slot, m], ra_sem.at[h, slot, m]
        else:
            dst, recv = sum_b.at[h, p, slot, m], rb_sem.at[h, p, slot, m]
        return remote(
            src, dst, rs_sem.at[h, k + p, s, m], recv, {"grp": g + 2 * away(s), "dev": l}
        )

    def final_copy(h, m):
        return remote(
            sums(h, 1, 1, z * parts + m),
            land_b.at[h, m],
            fs_sem.at[h, m],
            fr_sem.at[h, m],
            near(h),
        )

    barrier = pltpu.get_barrier_semaphore()

    def greet(device):
        pl.semaphore_signal(barrier, inc=1, device_id=device, device_id_type=MESH)

    @pl.when(z > 0)
    def _():
        greet({"grp": g - 2, "dev": l})

    @pl.when(z < depth - 1)
    def _():
        greet({"grp": g + 2, "dev": l})

    greet(peer(0, 2))
    for h in range(2):
        greet(peer(h, 1))
        greet(peer(h, 3))

    ins = []
    for h, src in ((0, tok_hbm), (1, cot_hbm)):
        for m in range(parts):
            for k, low in ((1, cut), (0, 0)):
                copy = pltpu.make_async_copy(
                    src.at[pl.ds(m * rows_mb, rows_mb), pl.ds(low, size[k])],
                    dense[k].at[h, 0, z, m, :, pl.ds(0, size[k])],
                    in_sem.at[2 * h + k, m],
                )
                copy.start()
                ins.append(copy)
    loads = [
        pltpu.make_async_copy(src, dst, w_sem.at[n])
        for n, (src, dst) in enumerate(
            ((gate_hbm, gate_ref), (up_hbm, up_ref), (down_hbm, down_ref))
        )
    ]
    for load in loads:
        load.start()

    row = lax.broadcasted_iota(jnp.int32, (rows, LANES), 0)
    lane = lax.broadcasted_iota(jnp.int32, (rows, LANES), 1)
    ids = ids_ref[...]
    mix = mix_ref[...].astype(f32)
    weight = jnp.zeros((rows, LANES), f32)
    named = jnp.zeros((rows, LANES), f32)
    for k in range(ids.shape[1]):
        expert_id = ids[:, k : k + 1]
        weight = weight + jnp.where(lane == expert_id, mix[:, k : k + 1], 0.0)
        named = named + jnp.where(lane == expert_id + experts, 1.0, 0.0)
    lives = live_ref[...]
    alive = jnp.zeros((rows, LANES), f32)
    for m in range(parts):
        first = m * rows_mb
        alive = alive + jnp.where(
            (row >= first) & (row < first + lives[0:1, m : m + 1]), 1.0, 0.0
        )
    row_a = lax.broadcasted_iota(jnp.int32, (rows, rows), 0)
    row_b = lax.broadcasted_iota(jnp.int32, (rows, rows), 1)
    before = jnp.where(
        (row_a > row_b) & (lax.div(row_a, rows_mb) == lax.div(row_b, rows_mb)), 1.0, 0.0
    ).astype(bf16)
    rank = jnp.dot(before, named.astype(bf16), preferred_element_type=f32)
    routes = jnp.where(lane < experts, weight * alive, rank).astype(bf16)
    for h in range(2):
        for m in range(parts):
            dense_a[h, 0, z, m, :, cut : cut + LANES] = routes[m * rows_mb : (m + 1) * rows_mb]

    lane_k = lax.broadcasted_iota(jnp.int32, (LANES, slots), 0)
    slot_k = lax.broadcasted_iota(jnp.int32, (LANES, slots), 1)
    quad = lax.div(slot_k, pair)
    owner = 2 * z + core + lax.div(quad, 2) * (1 - 2 * core)
    for h in range(2):
        target = owner * peers + jnp.where(lax.rem(quad, 2) == 1, flips[h], l)
        hot_ref[h, 0] = jnp.where(lane_k == target, 1.0, 0.0).astype(bf16)
        hot_ref[h, 1] = jnp.where(lane_k == target + experts, 1.0, 0.0).astype(bf16)
    row_s = lax.broadcasted_iota(jnp.int32, (both, slots), 0)
    col_s = lax.broadcasted_iota(jnp.int32, (both, slots), 1)
    slot_ref[...] = jnp.where(
        lax.div(row_s, rows_mb) == lax.rem(lax.div(col_s, per), 2), lax.rem(col_s, per), -1
    ).astype(f32)

    for copy in ins:
        copy.wait()
    pl.semaphore_wait(barrier, 5 + jnp.where(inner, 2, 1))

    def send_own(h, k, p, m):
        @pl.when(z < depth - 1)
        def _():
            spread_z(h, k, p, z, m, 1).start()

        @pl.when(z > 0)
        def _():
            spread_z(h, k, p, z, m, -1, True).start()

    def spread_own(k, p, m):
        for h in range(2):
            if p == 1:
                spread_p(h, 1, z, m).wait_recv()
            send_own(h, k, p, m)

    def pass_own(k, m):
        for h in range(2):
            spread_p(h, k, z, m).start()

    pass_own(1, 0)
    spread_own(0, 0, 0)
    spread_own(1, 0, 0)
    pass_own(0, 0)
    for m in range(1, parts):
        pass_own(1, m)
    for load in loads:
        load.wait()

    def arrive(k, p, s, m):
        for h in range(2):
            copy = spread_z(h, k, p, s, m, -away(s))
            copy.wait_recv()
            if k == 0:
                spread_p(h, 0, s, m).start()

            @pl.when(inner)
            def _(copy=copy):
                copy.start()

    def select(h, t, s, m):
        spread_p(h, 0, s, m).wait_recv()
        routes = dense_a[h, :, s, m, :, cut : cut + LANES].reshape(both, LANES)
        weights = jnp.dot(routes, hot_ref[h, 0], preferred_element_type=f32)
        ranks = jnp.dot(routes, hot_ref[h, 1], preferred_element_type=f32)
        weights = jnp.where(ranks == slot_ref[...], weights, 0.0)
        weight_ref[h, t] = weights.astype(bf16)
        pick = jnp.where(weights != 0.0, 1.0, 0.0).T.astype(bf16)
        for k, low in ((0, 0), (1, cut)):
            span = slice(low, low + size[k])
            placed = jnp.dot(
                pick,
                dense[k][h, :, s, m, :, 0 : size[k]].reshape(both, size[k]),
                preferred_element_type=f32,
            ).astype(bf16)
            kept = placed[0:pair].reshape(2, per, size[k])
            if h == 0:
                moved_x[t, 0, 0, :, :, span] = kept
            else:
                moved_dy[t, 0, :, 0, :, span] = kept
            send_ref[h, t, 2:8, :, span] = placed[pair:slots].reshape(6, per, size[k])
        for q in range(1, 4):
            select_copy(h, t, q).start()

    def expert(t):
        for h in range(2):
            for q in range(1, 4):
                select_copy(h, t, q).wait_recv()
        rows_x = moved_x[t].reshape(slots, width)
        rows_dy = moved_dy[t].reshape(slots, width)
        gate_pre = jnp.dot(rows_x, gate_ref[...], preferred_element_type=f32)
        up_pre = jnp.dot(rows_x, up_ref[...], preferred_element_type=f32)
        act_grad = lax.dot_general(
            rows_dy, down_ref[...], TRANS_RHS, preferred_element_type=f32
        )
        sig = jax.nn.sigmoid(gate_pre)
        gate_act = gate_pre * sig
        act = (gate_act * up_pre).astype(bf16)
        gate_grad = (act_grad * up_pre * sig * (1.0 + gate_pre * (1.0 - sig))).astype(bf16)
        up_grad = (act_grad * gate_act).astype(bf16)
        expert_out = jnp.dot(act, down_ref[...], preferred_element_type=f32)
        moved_x[t] = expert_out.astype(bf16).reshape(2, 2, 2, per, width)
        for q in range(1, 4):
            back_copy(0, t, q).start()
        expert_grad = lax.dot_general(
            gate_grad, gate_ref[...], TRANS_RHS, preferred_element_type=f32
        ) + lax.dot_general(up_grad, up_ref[...], TRANS_RHS, preferred_element_type=f32)
        moved_dy[t] = expert_grad.astype(bf16).reshape(2, 2, 2, per, width)
        for q in range(1, 4):
            back_copy(1, t, q).start()
        back_ref[0, t, 0] = moved_x[t, 0, 0]
        back_ref[1, t, 0] = moved_dy[t, 0, :, 0]

    def combine(h, t, s, m):
        for q in range(1, 4):
            back_copy(h, t, q).wait_recv()
            select_copy(h, t, q).wait_send()
        send_ref[h, t] = (
            jnp.dot(
                weight_ref[h, t],
                back_ref[h, t].reshape(slots, width),
                preferred_element_type=f32,
            )
            .astype(bf16)
            .reshape(2 * blocks, per, width)
        )
        pair_copy(h, t).start()

        @pl.when((s != z) & outer)
        def _():
            for p in range(2):
                onward(h, 1, p, s, m, sums(h, 1, p, t)).start()

    def pair_sum(h, t, s, m):
        pair_copy(h, t).wait_recv()
        kept = sums(h, 0, 0, t)
        kept[...] = (kept[...].astype(f32) + land_a[h, t].astype(f32)).astype(bf16)

        @pl.when((s != z) & outer)
        def _():
            onward(h, 0, 0, s, m, kept).start()

    def summed(h, k, p, slot, m):
        if k == 0:
            return sum_a.at[h, slot, m], ra_sem.at[h, slot, m]
        return sum_b.at[h, p, slot, m], rb_sem.at[h, p, slot, m]

    def landing(h, k, p, slot, m):
        ref, recv = summed(h, k, p, slot, m)
        remote(ref, ref, fs_sem.at[h, m], recv, near(h)).wait_recv()
        return ref

    def reduce(k, p, t, s, m):
        for h in range(2):
            ref = landing(h, k, p, s, m)
            ref[...] = (
                ref[...].astype(f32) + sums(h, k, p, t)[...].astype(f32)
            ).astype(bf16)
            onward(h, k, p, s, m, ref).start()

    def gather(h, k, p, t, m):
        first = jnp.where(z == depth - 1, depth, z)
        total = sums(h, k, p, t)[...].astype(f32) + landing(h, k, p, first, m)[...].astype(f32)
        ref, recv = summed(h, k, p, depth, m)

        @pl.when(inner)
        def _():
            landing(h, k, p, depth, m)

        return total + jnp.where(inner, ref[...].astype(f32), 0.0)

    def final(t, m):
        for h in range(2):
            sums(h, 1, 1, t)[...] = gather(h, 1, 1, t, m).astype(bf16)
            final_copy(h, m).start()

    def finish(t, m):
        span = pl.ds(m * rows_mb, rows_mb)
        for h in range(2):
            outs[h][span, 0:cut] = gather(h, 0, 0, t, m).astype(bf16).reshape(rows_mb, cut)
            total = gather(h, 1, 0, t, m)
            final_copy(h, m).wait_recv()
            outs[h][span, cut:width] = (
                (total + land_b[h, m].astype(f32)).astype(bf16).reshape(rows_mb, rest)
            )

    words = plan_words(depth, parts)
    held = [
        sum(jnp.where(z == k, words[k][b], 0) for k in range(depth))
        for b in range(len(words[0]))
    ]

    def run(code):
        kind = lax.div(code, count)
        t = lax.rem(code, count)
        s = lax.div(t, parts)
        m = lax.rem(t, parts)

        def on(low, high=None):
            return pl.when(kind == low if high is None else (kind >= low) & (kind <= high))

        @on(ARRIVE, ARRIVE + 2)
        def _():
            for n, (k, p) in enumerate(PIECES):
                on(ARRIVE + n)(lambda k=k, p=p: arrive(k, p, s, m))

        for h in range(2):
            on(SELECT + h)(lambda h=h: select(h, t, s, m))
        on(EXPERT)(lambda: expert(t))

        @on(COMBINE, PAIR_SUM + 1)
        def _():
            for h in range(2):
                on(COMBINE + h)(lambda h=h: combine(h, t, s, m))
                on(PAIR_SUM + h)(lambda h=h: pair_sum(h, t, s, m))

        @on(REDUCE, REDUCE + 2)
        def _():
            for n, (k, p) in enumerate(PIECES):
                on(REDUCE + n)(lambda k=k, p=p: reduce(k, p, t, s, m))

        @on(OWN, FINISH)
        def _():
            for n, (k, p) in enumerate(PIECES):
                on(OWN + n)(lambda k=k, p=p: spread_own(k, p, m))
            on(PASS_OWN)(lambda: pass_own(0, m))
            on(FINAL)(lambda: final(t, m))
            on(FINISH)(lambda: finish(t, m))

    def block(b, carry):
        word = sum(jnp.where(b == k, held[k], 0) for k in range(len(held)))

        def one(n, word):
            run(lax.rem(word, KINDS * count))
            return lax.div(word, KINDS * count)

        lax.fori_loop(0, PACKED, one, word)
        return carry

    lax.fori_loop(0, len(held), block, 0)

    def drain(t, carry):
        s = lax.div(t, parts)
        m = lax.rem(t, parts)
        for h in range(2):
            spread_p(h, 0, s, m).wait_send()
            pair_copy(h, t).wait_send()
            for q in range(1, 4):
                back_copy(h, t, q).wait_send()

            @pl.when(s == z)
            def _(h=h):
                spread_p(h, 1, s, m).wait_send()
                for k, p in PIECES:

                    @pl.when(z < depth - 1)
                    def _(k=k, p=p):
                        spread_z(h, k, p, z, m, 1).wait_send()

                    @pl.when(z > 0)
                    def _(k=k, p=p):
                        spread_z(h, k, p, z, m, -1, True).wait_send()

            @pl.when(s != z)
            def _(h=h):
                for k, p in PIECES:
                    onward(h, k, p, s, m, sums(h, k, p, t)).wait_send()

                    @pl.when(inner)
                    def _(k=k, p=p):
                        spread_z(h, k, p, s, m, -away(s)).wait_send()

        return carry

    lax.fori_loop(0, count, drain, 0)
    for m in range(parts):
        for h in range(2):
            final_copy(h, m).wait_send()


def plane_cut(width):
    blocks = width // LANES
    return max(1, blocks * 5 // 9) * LANES


def plane_local(
    tokens, cotangent, expert_ids, combine_weights, live_counts, gate_weight, up_weight, down_weight
):
    groups = lax.axis_size("grp")
    peers = lax.axis_size("dev")
    experts = groups * peers
    depth = groups // 2
    rows, width = tokens.shape
    hidden = gate_weight.shape[2]
    parts = live_counts.shape[1]
    rows_mb = rows // parts
    per = rows_mb * expert_ids.shape[1] // experts
    cut = plane_cut(width)
    blocks = rows_mb // per
    rest = width - cut
    count = depth * parts
    slots = 8 * per
    vmem = pl.BlockSpec(memory_space=pltpu.VMEM)
    anywhere = pl.BlockSpec(memory_space=pl.ANY)
    dma = pltpu.SemaphoreType.DMA
    bf16 = jnp.bfloat16
    return pl.pallas_call(
        functools.partial(plane_kernel, groups, parts, experts, per, cut),
        out_shape=(
            jax.ShapeDtypeStruct((rows, width), bf16),
            jax.ShapeDtypeStruct((rows, width), bf16),
        ),
        in_specs=[anywhere] * 2 + [vmem] * 3 + [anywhere] * 3,
        out_specs=(vmem, vmem),
        scratch_shapes=[
            pltpu.VMEM((width, hidden), bf16),
            pltpu.VMEM((width, hidden), bf16),
            pltpu.VMEM((hidden, width), bf16),
            pltpu.VMEM((2, 2, depth, parts, rows_mb, cut + LANES), bf16),
            pltpu.VMEM((2, 2, depth, parts, rows_mb, rest), bf16),
            pltpu.VMEM((2, 2, LANES, slots), bf16),
            pltpu.VMEM((2 * rows_mb, slots), jnp.float32),
            pltpu.VMEM((2, count, 2 * rows_mb, slots), bf16),
            pltpu.VMEM((2, count, 8, per, width), bf16),
            pltpu.VMEM((count, 2, 2, 2, per, width), bf16),
            pltpu.VMEM((count, 2, 2, 2, per, width), bf16),
            pltpu.VMEM((2, count, 4, 2, per, width), bf16),
            pltpu.VMEM((2, count, blocks, per, cut), bf16),
            pltpu.VMEM((2, parts, blocks, per, rest), bf16),
            pltpu.VMEM((2, depth + 1, parts, blocks, per, cut), bf16),
            pltpu.VMEM((2, 2, depth + 1, parts, blocks, per, rest), bf16),
            dma((3,)),
            dma((4, parts)),
            dma((4, 2, depth, parts)),
            dma((4, 2, depth, parts)),
            dma((4, 2, parts)),
            dma((4, depth, parts)),
            dma((2, count, 4)),
            dma((2, count, 4)),
            dma((2, count, 4)),
            dma((2, count, 4)),
            dma((2, count)),
            dma((2, count)),
            dma((2, depth + 1, parts)),
            dma((2, 2, depth + 1, parts)),
            dma((2, 3, depth, parts)),
            dma((2, parts)),
            dma((2, parts)),
        ],
        compiler_params=pltpu.CompilerParams(
            collective_id=0, has_side_effects=True, vmem_limit_bytes=65 * 1024 * 1000
        ),
    )(
        tokens,
        cotangent,
        expert_ids,
        combine_weights,
        live_counts,
        gate_weight[0],
        up_weight[0],
        down_weight[0],
    )


def local(*args):
    groups = lax.axis_size("grp")
    peers = lax.axis_size("dev")
    depth = groups // 2
    fits = 2 * groups * peers <= LANES
    planned = depth in PLANS and args[4].shape[1] == PLAN_PARTS
    if peers == 4 and groups % 2 == 0 and planned and fits:
        return plane_local(*args)
    return general_local(*args)


def solution(mesh):
    spec2 = P(("grp", "dev"), None)
    spec3 = P(("grp", "dev"), None, None)
    return jax.shard_map(
        local,
        mesh=mesh,
        in_specs=(spec2,) * 5 + (spec3,) * 3,
        out_specs=(spec2, spec2),
        check_vma=False,
    )
```

```python
import functools

import jax
import jax.numpy as jnp
from jax import lax
from jax.experimental import pallas as pl
from jax.experimental.pallas import tpu as pltpu
from jax.sharding import PartitionSpec as P

PAIR = 2
LAG_EXPERT = 1
LAG_RETURN = 2
MESH = pl.DeviceIdType.MESH
TRANS_RHS = (((1,), (1,)), ((), ()))


def xor(a, b, size):
    out = 0
    bit = 1
    while bit < size:
        out = out + ((a // bit + b // bit) % 2) * bit
        bit *= 2
    return out


def chunk_order(groups):
    if groups < 8:
        return list(range(groups))
    return [0, 4, 2] + list(range(5, groups)) + [3, 1]


def distance_of(unit, parts, groups):
    i = unit // parts
    out = 0
    for k, value in enumerate(chunk_order(groups)):
        out = out + value * ((i + groups - k) // groups - (i + groups - k - 1) // groups)
    return out


def moe_kernel(
    groups,
    peers,
    joined,
    parts,
    tok_ref,
    cot_ref,
    pick_ref,
    slot_ref,
    sum_ref,
    gate_hbm,
    up_hbm,
    down_hbm,
    out_ref,
    grad_ref,
    gate_ref,
    up_ref,
    down_ref,
    zsend,
    zrecv,
    zback,
    xysend,
    xyrecv,
    xyback,
    w_sem,
    zs_sem,
    zr_sem,
    bs_sem,
    br_sem,
    ds_sem,
    dr_sem,
    rs_sem,
    rr_sem,
):
    g = lax.axis_index("grp")
    l = lax.axis_index("dev")
    width = tok_ref.shape[1]
    wide = 2 * width
    units = groups * parts
    chunks = units // joined
    group_rows = zrecv.shape[1]
    slots = slot_ref.shape[2]
    peer_rows = slots // peers

    barrier = pltpu.get_barrier_semaphore()
    for k in range(1, groups):
        pl.semaphore_signal(
            barrier, inc=1, device_id={"grp": xor(g, k, groups)}, device_id_type=MESH
        )
    for q in range(1, peers):
        pl.semaphore_signal(
            barrier, inc=1, device_id={"dev": xor(l, q, peers)}, device_id_type=MESH
        )

    loads = [
        pltpu.make_async_copy(src, dst, w_sem.at[n])
        for n, (src, dst) in enumerate(
            ((gate_hbm, gate_ref), (up_hbm, up_ref), (down_hbm, down_ref))
        )
    ]
    for load in loads:
        load.start()

    def z_copy(i):
        return pltpu.make_async_remote_copy(
            src_ref=zsend.at[i],
            dst_ref=zrecv.at[i],
            send_sem=zs_sem.at[i],
            recv_sem=zr_sem.at[i],
            device_id={"grp": xor(g, distance_of(i, parts, groups), groups)},
            device_id_type=MESH,
        )

    def z_back(i):
        return pltpu.make_async_remote_copy(
            src_ref=zrecv.at[i, :, pl.ds(0, wide)],
            dst_ref=zback.at[i],
            send_sem=bs_sem.at[i],
            recv_sem=br_sem.at[i],
            device_id={"grp": xor(g, distance_of(i, parts, groups), groups)},
            device_id_type=MESH,
        )

    def xy_copy(c, q):
        return pltpu.make_async_remote_copy(
            src_ref=xysend.at[c, q],
            dst_ref=xyrecv.at[c, q],
            send_sem=ds_sem.at[c, q],
            recv_sem=dr_sem.at[c, q],
            device_id={"dev": xor(l, q, peers)},
            device_id_type=MESH,
        )

    def xy_back(c, q):
        return pltpu.make_async_remote_copy(
            src_ref=xyrecv.at[c, q],
            dst_ref=xyback.at[c, q],
            send_sem=rs_sem.at[c, q],
            recv_sem=rr_sem.at[c, q],
            device_id={"dev": xor(l, q, peers)},
            device_id_type=MESH,
        )

    def fill(i, target):
        pick = pick_ref[i]
        for source, low in ((tok_ref, 0), (cot_ref, width)):
            target[i, :, low : low + width] = jnp.dot(
                pick, source[...], preferred_element_type=jnp.float32
            ).astype(jnp.bfloat16)
        target[i, :, wide : wide + slots] = jnp.dot(
            pick, slot_ref[i // parts], preferred_element_type=jnp.float32
        ).astype(jnp.bfloat16)

    for i in range(parts):
        fill(i, zrecv)

    def chunk_weights(c):
        block = zrecv[pl.ds(c * joined, joined), :, wide : wide + slots]
        return block.reshape(joined * group_rows, slots)

    def place(c):
        for j in range(joined):
            i = c * joined + j

            @pl.when(i >= parts)
            def _(i=i):
                z_copy(i).wait_recv()

        weights = chunk_weights(c).astype(jnp.float32)
        select = jnp.where(weights != 0.0, 1.0, 0.0).T.astype(jnp.bfloat16)
        rows = zrecv[pl.ds(c * joined, joined), :, 0:wide].reshape(joined * group_rows, wide)
        placed = jnp.dot(select, rows, preferred_element_type=jnp.float32).astype(jnp.bfloat16)
        for q in range(1, peers):
            xysend[c, q] = placed[q * peer_rows : (q + 1) * peer_rows]
            xy_copy(c, q).start()
        xyrecv[c, 0] = placed[0:peer_rows]

    def expert(c):
        @pl.when(c == 0)
        def _():
            for load in loads:
                load.wait()

        for q in range(1, peers):
            xy_copy(c, q).wait_recv()
        rows_x = xyrecv[c, :, :, 0:width].reshape(slots, width)
        rows_dy = xyrecv[c, :, :, width:wide].reshape(slots, width)
        gate_pre = jnp.dot(rows_x, gate_ref[...], preferred_element_type=jnp.float32)
        up_pre = jnp.dot(rows_x, up_ref[...], preferred_element_type=jnp.float32)
        act_grad = lax.dot_general(
            rows_dy, down_ref[...], TRANS_RHS, preferred_element_type=jnp.float32
        )
        sig = jax.nn.sigmoid(gate_pre)
        gate_act = gate_pre * sig
        act = (gate_act * up_pre).astype(jnp.bfloat16)
        gate_grad = (act_grad * up_pre * sig * (1.0 + gate_pre * (1.0 - sig))).astype(jnp.bfloat16)
        up_grad = (act_grad * gate_act).astype(jnp.bfloat16)
        expert_out = jnp.dot(act, down_ref[...], preferred_element_type=jnp.float32)
        xyrecv[c, :, :, 0:width] = expert_out.astype(jnp.bfloat16).reshape(peers, peer_rows, width)
        expert_grad = lax.dot_general(
            gate_grad, gate_ref[...], TRANS_RHS, preferred_element_type=jnp.float32
        ) + lax.dot_general(up_grad, up_ref[...], TRANS_RHS, preferred_element_type=jnp.float32)
        xyrecv[c, :, :, width:wide] = expert_grad.astype(jnp.bfloat16).reshape(
            peers, peer_rows, width
        )
        for q in range(1, peers):
            xy_back(c, q).start()
        xyback[c, 0] = xyrecv[c, 0]

    def combine(c):
        for q in range(1, peers):
            xy_back(c, q).wait_recv()
        weights = chunk_weights(c)
        pairs = jnp.dot(
            weights, xyback[c].reshape(slots, wide), preferred_element_type=jnp.float32
        ).astype(jnp.bfloat16)
        zrecv[pl.ds(c * joined, joined), :, 0:wide] = pairs.reshape(joined, group_rows, wide)
        for j in range(joined):
            i = c * joined + j

            @pl.when(i >= parts)
            def _():
                z_back(i).start()

    early = min(1, parts // joined)
    pl.semaphore_wait(barrier, groups + peers - 2)
    for c in range(early):
        place(c)
    fill(parts, zsend)

    def send_step(i, carry):
        fill(i, zsend)
        z_copy(i - 1).start()
        return carry

    lax.fori_loop(parts + 1, units, send_step, 0)
    z_copy(units - 1).start()

    def step(t, carry):
        @pl.when((t >= early) & (t < chunks))
        def _():
            place(t)

        @pl.when((t >= LAG_EXPERT) & (t < chunks + LAG_EXPERT))
        def _():
            expert(t - LAG_EXPERT)

        @pl.when(t >= LAG_RETURN)
        def _():
            combine(t - LAG_RETURN)

        return carry

    lax.fori_loop(0, chunks + LAG_RETURN, step, 0)

    for i in range(parts):
        zback[i] = zrecv[i, :, 0:wide]

    def finish_step(i, carry):
        z_back(i).wait_recv()
        return carry

    lax.fori_loop(parts, units, finish_step, 0)
    for target, low in ((out_ref, 0), (grad_ref, width)):
        target[...] = jnp.dot(
            sum_ref[...],
            zback[:, :, low : low + width].reshape(units * group_rows, width),
            preferred_element_type=jnp.float32,
        ).astype(jnp.bfloat16)

    def drain_z(i, carry):
        z_copy(i).wait_send()
        z_back(i).wait_send()
        return carry

    lax.fori_loop(parts, units, drain_z, 0)

    def drain_xy(c, carry):
        for q in range(1, peers):
            xy_copy(c, q).wait_send()
            xy_back(c, q).wait_send()
        return carry

    lax.fori_loop(0, chunks, drain_xy, 0)


def routing(expert_ids, combine_weights, live_counts, groups, peers, joined):
    rows, top_count = expert_ids.shape
    parts = live_counts.shape[1]
    rows_mb = rows // parts
    experts = groups * peers
    units = groups * parts
    per_expert = rows_mb * top_count // experts
    per_group = per_expert * peers // PAIR
    g = lax.axis_index("grp")
    l = lax.axis_index("dev")
    relative = ((expert_ids // peers) ^ g) * peers + ((expert_ids % peers) ^ l)
    order = jnp.array(chunk_order(groups), jnp.int32)
    wanted = (order[:, None] * peers + jnp.arange(peers, dtype=jnp.int32)).reshape(-1)
    hit = relative[:, :, None] == wanted
    member = jnp.any(hit, axis=1)
    weight = jnp.sum(
        jnp.where(hit, combine_weights.astype(jnp.float32)[:, :, None], 0.0), axis=1
    )
    index = jnp.arange(rows, dtype=jnp.int32)
    part = index // rows_mb
    live = (index % rows_mb) < jnp.repeat(live_counts[0], rows_mb)
    weight = jnp.where(live[:, None], weight, 0.0).astype(jnp.bfloat16)
    in_group = jnp.any(member.reshape(rows, groups, peers), axis=2)
    both = jnp.concatenate([member, in_group], axis=1).astype(jnp.bfloat16)
    before = (
        (index[:, None] > index[None, :]) & (part[:, None] == part[None, :])
    ).astype(jnp.bfloat16)
    rank = jnp.dot(before, both, preferred_element_type=jnp.float32).astype(jnp.int32)
    expert_rank, group_rank = rank[:, :experts], rank[:, experts:]
    group_slot = jnp.where(in_group, group_rank + part[:, None] * per_group, -1)
    unit_rows = jnp.arange(parts * per_group, dtype=jnp.int32)
    pick = (
        (group_slot.T[:, None, :] == unit_rows[None, :, None])
        .astype(jnp.bfloat16)
        .reshape(units, per_group, rows)
    )
    total = (
        (group_slot[:, :, None] == unit_rows)
        .astype(jnp.bfloat16)
        .reshape(rows, units * per_group)
    )
    width = joined * per_expert
    offset = jnp.arange(groups, dtype=jnp.int32)[None, :] * parts + part[:, None]
    expert_slot = expert_rank.reshape(rows, groups, peers) + (
        offset % joined * per_expert
    )[..., None]
    expert_slot = expert_slot.transpose(1, 0, 2)[..., None]
    slot = jnp.where(
        expert_slot == jnp.arange(width, dtype=jnp.int32),
        weight.reshape(rows, groups, peers).transpose(1, 0, 2)[..., None],
        jnp.zeros((), jnp.bfloat16),
    ).reshape(groups, rows, peers * width)
    return pick, slot, total


def general_local(
    tokens, cotangent, expert_ids, combine_weights, live_counts, gate_weight, up_weight, down_weight
):
    groups = lax.axis_size("grp")
    peers = lax.axis_size("dev")
    rows, width = tokens.shape
    hidden = gate_weight.shape[2]
    parts = live_counts.shape[1]
    units = groups * parts
    per_expert = rows // parts * expert_ids.shape[1] // (groups * peers)
    per_group = per_expert * peers // PAIR
    joined = max(1, 16 // per_expert)
    chunks = units // joined
    peer_rows = joined * per_expert
    slots = peers * peer_rows
    wide = 2 * width
    pick, slot, total = routing(
        expert_ids, combine_weights, live_counts, groups, peers, joined
    )
    vmem = pl.BlockSpec(memory_space=pltpu.VMEM)
    anywhere = pl.BlockSpec(memory_space=pl.ANY)
    dma = pltpu.SemaphoreType.DMA
    bf16 = jnp.bfloat16
    return pl.pallas_call(
        functools.partial(moe_kernel, groups, peers, joined, parts),
        out_shape=(
            jax.ShapeDtypeStruct((rows, width), bf16),
            jax.ShapeDtypeStruct((rows, width), bf16),
        ),
        in_specs=[vmem] * 5 + [anywhere] * 3,
        out_specs=(vmem, vmem),
        scratch_shapes=[
            pltpu.VMEM((width, hidden), bf16),
            pltpu.VMEM((width, hidden), bf16),
            pltpu.VMEM((hidden, width), bf16),
            pltpu.VMEM((units, per_group, wide + slots), bf16),
            pltpu.VMEM((units, per_group, wide + slots), bf16),
            pltpu.VMEM((units, per_group, wide), bf16),
            pltpu.VMEM((chunks, peers, peer_rows, wide), bf16),
            pltpu.VMEM((chunks, peers, peer_rows, wide), bf16),
            pltpu.VMEM((chunks, peers, peer_rows, wide), bf16),
            dma((3,)),
            dma((units,)),
            dma((units,)),
            dma((units,)),
            dma((units,)),
            dma((chunks, peers)),
            dma((chunks, peers)),
            dma((chunks, peers)),
            dma((chunks, peers)),
        ],
        compiler_params=pltpu.CompilerParams(
            collective_id=0, has_side_effects=True, vmem_limit_bytes=65 * 1024 * 1000
        ),
    )(
        tokens,
        cotangent,
        pick,
        slot,
        total,
        gate_weight[0],
        up_weight[0],
        down_weight[0],
    )


LANES = 128
SETTLE = 2


PIECES = ((0, 0), (1, 0), (1, 1))
ARRIVE, SELECT, EXPERT, COMBINE, PAIR_SUM, REDUCE = 0, 3, 5, 6, 8, 10
OWN, PASS_OWN, FINAL, FINISH, IDLE = 13, 16, 17, 18, 19
KINDS = 32
PACKED = 3
PLAN_PARTS = 2
PLAN_4 = (
    (
        129, 2, 120, 105, 24, 32, 10, 121, 18, 34, 26, 40, 4, 42, 113, 20, 12, 28, 36, 6, 58,
        50, 44, 7, 74, 14, 66, 22, 52, 60, 30, 15, 38, 76, 68, 23, 31, 39, 46, 47, 3, 54, 19,
        62, 55, 5, 63, 11, 27, 13, 70, 78, 35, 21, 29, 79, 71, 37, 43, 45, 33, 25, 59, 53, 48,
        61, 41, 69, 77, 51, 56, 49, 75, 57, 137, 64, 67, 136, 72, 65, 73, 145, 144,
    ),
    (
        122, 26, 34, 4, 0, 20, 12, 28, 36, 8, 6, 16, 32, 1, 17, 24, 14, 44, 7, 9, 22, 30, 38,
        40, 15, 23, 31, 39, 60, 115, 107, 56, 33, 123, 48, 47, 46, 63, 5, 55, 13, 25, 131, 54,
        52, 100, 62, 21, 72, 92, 102, 41, 76, 94, 37, 35, 29, 95, 79, 78, 49, 70, 103, 27, 96,
        86, 71, 45, 87, 68, 88, 42, 64, 53, 57, 80, 61, 84, 97, 89, 43, 93, 101, 58, 73, 50,
        138, 65, 51, 81, 59, 77, 69, 85, 74, 139, 67, 66, 75, 146, 147,
    ),
)
PLANS = {4: PLAN_4}


def plan_words(depth, parts):
    count = depth * parts
    base = KINDS * count
    orders = []
    for z in range(depth):
        codes = list(PLANS[depth][min(z, depth - 1 - z)])
        if 2 * z >= depth:
            codes = [
                kind - kind % count + (depth - 1 - kind % count // parts) * parts + kind % parts
                for kind in codes
            ]
        orders.append(codes)
    length = max(len(codes) for codes in orders)
    length += -length % PACKED
    words = []
    for codes in orders:
        codes = codes + [IDLE * count] * (length - len(codes))
        words.append(
            [
                sum(codes[b + n] * base**n for n in range(PACKED))
                for b in range(0, length, PACKED)
            ]
        )
    return words


def plane_kernel(
    groups,
    parts,
    experts,
    per,
    cut,
    tok_hbm,
    cot_hbm,
    ids_ref,
    mix_ref,
    live_ref,
    gate_hbm,
    up_hbm,
    down_hbm,
    out_ref,
    grad_ref,
    gate_ref,
    up_ref,
    down_ref,
    dense_a,
    dense_b,
    hot_ref,
    slot_ref,
    weight_ref,
    send_ref,
    moved_x,
    moved_dy,
    back_ref,
    land_a,
    land_b,
    sum_a,
    sum_b,
    w_sem,
    in_sem,
    agr_sem,
    agz_sem,
    agd_sem,
    agp_sem,
    ss_sem,
    sr_sem,
    bs_sem,
    br_sem,
    ps_sem,
    pr_sem,
    ra_sem,
    rb_sem,
    rs_sem,
    fs_sem,
    fr_sem,
):
    g = lax.axis_index("grp")
    l = lax.axis_index("dev")
    depth = groups // 2
    z = g // 2
    core = g % 2
    peers = experts // groups
    rows_mb = dense_a.shape[4]
    rows = rows_mb * parts
    width = down_ref.shape[1]
    rest = width - cut
    count = depth * parts
    pair = 2 * per
    blocks = rows_mb // per
    slots = 4 * pair
    both = 2 * rows_mb
    f32 = jnp.float32
    bf16 = jnp.bfloat16
    inner = (z > 0) & (z < depth - 1)
    outer = (z == 0) | (z == depth - 1)
    dense = (dense_a, dense_b)
    size = (cut, rest)
    outs = (out_ref, grad_ref)

    flips = (l + 2 - 4 * (l // 2), l + 1 - 2 * (l % 2))

    def near(h):
        return {"grp": g, "dev": flips[1 - h]}

    def peer(h, q):
        return {
            "grp": g + (q // 2) * (1 - 2 * core),
            "dev": flips[h] if q % 2 else l,
        }

    def remote(src, dst, send, recv, device):
        return pltpu.make_async_remote_copy(
            src_ref=src,
            dst_ref=dst,
            send_sem=send,
            recv_sem=recv,
            device_id=device,
            device_id_type=MESH,
        )

    def spread_z(h, k, p, s, m, d, second=False):
        slot = dense[k].at[h, p, s, m]
        send = agd_sem.at[2 * h + k, p, m] if second else agz_sem.at[2 * h + k, p, s, m]
        return remote(
            slot, slot, send, agr_sem.at[2 * h + k, p, s, m], {"grp": g + 2 * d, "dev": l}
        )

    def spread_p(h, k, s, m):
        return remote(
            dense[k].at[h, 0, s, m],
            dense[k].at[h, 1, s, m],
            agp_sem.at[2 * h + k, s, m],
            agr_sem.at[2 * h + k, 1, s, m],
            near(h),
        )

    def moved(h, t, q):
        if h == 0:
            return moved_x.at[t, q // 2, q % 2]
        return moved_dy.at[t, q // 2, :, q % 2]

    def select_copy(h, t, q):
        return remote(
            send_ref.at[h, t, pl.ds(2 * q, 2)],
            moved(h, t, q),
            ss_sem.at[h, t, q],
            sr_sem.at[h, t, q],
            peer(h, q),
        )

    def back_copy(h, t, q):
        return remote(
            moved(h, t, q),
            back_ref.at[h, t, q],
            bs_sem.at[h, t, q],
            br_sem.at[h, t, q],
            peer(h, q),
        )

    def sums(h, k, p, t):
        low = 0 if k == 0 else cut
        return send_ref.at[h, t, pl.ds(p * blocks, blocks), :, pl.ds(low, size[k])]

    def pair_copy(h, t):
        return remote(
            sums(h, 0, 1, t), land_a.at[h, t], ps_sem.at[h, t], pr_sem.at[h, t], near(h)
        )

    def away(s):
        return jnp.where(s > z, 1, -1)

    def onward(h, k, p, s, m, src):
        slot = jnp.where(s == z + 1, depth, s)
        if k == 0:
            dst, recv = sum_a.at[h, slot, m], ra_sem.at[h, slot, m]
        else:
            dst, recv = sum_b.at[h, p, slot, m], rb_sem.at[h, p, slot, m]
        return remote(
            src, dst, rs_sem.at[h, k + p, s, m], recv, {"grp": g + 2 * away(s), "dev": l}
        )

    def final_copy(h, m):
        return remote(
            sums(h, 1, 1, z * parts + m),
            land_b.at[h, m],
            fs_sem.at[h, m],
            fr_sem.at[h, m],
            near(h),
        )

    barrier = pltpu.get_barrier_semaphore()

    def greet(device):
        pl.semaphore_signal(barrier, inc=1, device_id=device, device_id_type=MESH)

    @pl.when(z > 0)
    def _():
        greet({"grp": g - 2, "dev": l})

    @pl.when(z < depth - 1)
    def _():
        greet({"grp": g + 2, "dev": l})

    greet(peer(0, 2))
    for h in range(2):
        greet(peer(h, 1))
        greet(peer(h, 3))

    ins = []
    for h, src in ((0, tok_hbm), (1, cot_hbm)):
        for m in range(parts):
            for k, low in ((1, cut), (0, 0)):
                copy = pltpu.make_async_copy(
                    src.at[pl.ds(m * rows_mb, rows_mb), pl.ds(low, size[k])],
                    dense[k].at[h, 0, z, m, :, pl.ds(0, size[k])],
                    in_sem.at[2 * h + k, m],
                )
                copy.start()
                ins.append(copy)
    loads = [
        pltpu.make_async_copy(src, dst, w_sem.at[n])
        for n, (src, dst) in enumerate(
            ((gate_hbm, gate_ref), (up_hbm, up_ref), (down_hbm, down_ref))
        )
    ]
    for load in loads:
        load.start()

    lane = lax.broadcasted_iota(jnp.int32, (LANES, rows), 0)
    row = lax.broadcasted_iota(jnp.int32, (LANES, rows), 1)
    ids = ids_ref[...]
    mix = mix_ref[...].astype(f32)
    weight = jnp.zeros((LANES, rows), f32)
    named = jnp.zeros((LANES, rows), f32)
    for k in range(ids.shape[0]):
        expert_id = ids[k : k + 1]
        weight = weight + jnp.where(lane == expert_id, mix[k : k + 1], 0.0)
        named = named + jnp.where(lane == expert_id + experts, 1.0, 0.0)
    lives = live_ref[...]
    alive = jnp.zeros((LANES, rows), f32)
    for m in range(parts):
        first = m * rows_mb
        alive = alive + jnp.where(
            (row >= first) & (row < first + lives[0:1, m : m + 1]), 1.0, 0.0
        )
    row_a = lax.broadcasted_iota(jnp.int32, (rows, rows), 1)
    row_b = lax.broadcasted_iota(jnp.int32, (rows, rows), 0)
    before = jnp.where(
        (row_a > row_b) & (lax.div(row_a, rows_mb) == lax.div(row_b, rows_mb)), 1.0, 0.0
    ).astype(bf16)
    rank = jnp.dot(named.astype(bf16), before, preferred_element_type=f32)
    routes = jnp.where(lane < experts, weight * alive, rank).T.astype(bf16)
    for h in range(2):
        for m in range(parts):
            dense_a[h, 0, z, m, :, cut : cut + LANES] = routes[m * rows_mb : (m + 1) * rows_mb]

    lane_k = lax.broadcasted_iota(jnp.int32, (LANES, slots), 0)
    slot_k = lax.broadcasted_iota(jnp.int32, (LANES, slots), 1)
    quad = lax.div(slot_k, pair)
    owner = 2 * z + core + lax.div(quad, 2) * (1 - 2 * core)
    for h in range(2):
        target = owner * peers + jnp.where(lax.rem(quad, 2) == 1, flips[h], l)
        hot_ref[h, 0] = jnp.where(lane_k == target, 1.0, 0.0).astype(bf16)
        hot_ref[h, 1] = jnp.where(lane_k == target + experts, 1.0, 0.0).astype(bf16)
    row_s = lax.broadcasted_iota(jnp.int32, (both, slots), 0)
    col_s = lax.broadcasted_iota(jnp.int32, (both, slots), 1)
    slot_ref[...] = jnp.where(
        lax.div(row_s, rows_mb) == lax.rem(lax.div(col_s, per), 2), lax.rem(col_s, per), -1
    ).astype(f32)

    for copy in ins:
        copy.wait()
    pl.semaphore_wait(barrier, 5 + jnp.where(inner, 2, 1))

    def send_own(h, k, p, m):
        @pl.when(z < depth - 1)
        def _():
            spread_z(h, k, p, z, m, 1).start()

        @pl.when(z > 0)
        def _():
            spread_z(h, k, p, z, m, -1, True).start()

    def spread_own(k, p, m):
        for h in range(2):
            if p == 1:
                spread_p(h, 1, z, m).wait_recv()
            send_own(h, k, p, m)

    def pass_own(k, m):
        for h in range(2):
            spread_p(h, k, z, m).start()

    pass_own(1, 0)
    spread_own(0, 0, 0)
    spread_own(1, 0, 0)
    pass_own(0, 0)
    for m in range(1, parts):
        pass_own(1, m)
    for load in loads:
        load.wait()

    def arrive(k, p, s, m):
        for h in range(2):
            copy = spread_z(h, k, p, s, m, -away(s))
            copy.wait_recv()
            if k == 0:
                spread_p(h, 0, s, m).start()

            @pl.when(inner)
            def _(copy=copy):
                copy.start()

    def select(h, t, s, m):
        spread_p(h, 0, s, m).wait_recv()
        routes = dense_a[h, :, s, m, :, cut : cut + LANES].reshape(both, LANES)
        weights = jnp.dot(routes, hot_ref[h, 0], preferred_element_type=f32)
        ranks = jnp.dot(routes, hot_ref[h, 1], preferred_element_type=f32)
        weights = jnp.where(ranks == slot_ref[...], weights, 0.0)
        weight_ref[h, t] = weights.astype(bf16)
        pick = jnp.where(weights != 0.0, 1.0, 0.0).T.astype(bf16)
        for k, low in ((0, 0), (1, cut)):
            span = slice(low, low + size[k])
            placed = jnp.dot(
                pick,
                dense[k][h, :, s, m, :, 0 : size[k]].reshape(both, size[k]),
                preferred_element_type=f32,
            ).astype(bf16)
            kept = placed[0:pair].reshape(2, per, size[k])
            if h == 0:
                moved_x[t, 0, 0, :, :, span] = kept
            else:
                moved_dy[t, 0, :, 0, :, span] = kept
            send_ref[h, t, 2:8, :, span] = placed[pair:slots].reshape(6, per, size[k])
        for q in range(1, 4):
            select_copy(h, t, q).start()

    def expert(t):
        for h in range(2):
            for q in range(1, 4):
                select_copy(h, t, q).wait_recv()
        rows_x = moved_x[t].reshape(slots, width)
        rows_dy = moved_dy[t].reshape(slots, width)
        gate_pre = jnp.dot(rows_x, gate_ref[...], preferred_element_type=f32)
        up_pre = jnp.dot(rows_x, up_ref[...], preferred_element_type=f32)
        act_grad = lax.dot_general(
            rows_dy, down_ref[...], TRANS_RHS, preferred_element_type=f32
        )
        sig = jax.nn.sigmoid(gate_pre)
        gate_act = gate_pre * sig
        act = (gate_act * up_pre).astype(bf16)
        gate_grad = (act_grad * up_pre * sig * (1.0 + gate_pre * (1.0 - sig))).astype(bf16)
        up_grad = (act_grad * gate_act).astype(bf16)
        expert_out = jnp.dot(act, down_ref[...], preferred_element_type=f32)
        moved_x[t] = expert_out.astype(bf16).reshape(2, 2, 2, per, width)
        for q in range(1, 4):
            back_copy(0, t, q).start()
        expert_grad = lax.dot_general(
            gate_grad, gate_ref[...], TRANS_RHS, preferred_element_type=f32
        ) + lax.dot_general(up_grad, up_ref[...], TRANS_RHS, preferred_element_type=f32)
        moved_dy[t] = expert_grad.astype(bf16).reshape(2, 2, 2, per, width)
        for q in range(1, 4):
            back_copy(1, t, q).start()
        back_ref[0, t, 0] = moved_x[t, 0, 0]
        back_ref[1, t, 0] = moved_dy[t, 0, :, 0]

    def combine(h, t, s, m):
        for q in range(1, 4):
            back_copy(h, t, q).wait_recv()
            select_copy(h, t, q).wait_send()
        send_ref[h, t] = (
            jnp.dot(
                weight_ref[h, t],
                back_ref[h, t].reshape(slots, width),
                preferred_element_type=f32,
            )
            .astype(bf16)
            .reshape(2 * blocks, per, width)
        )
        pair_copy(h, t).start()

        @pl.when((s != z) & outer)
        def _():
            for p in range(2):
                onward(h, 1, p, s, m, sums(h, 1, p, t)).start()

    def pair_sum(h, t, s, m):
        pair_copy(h, t).wait_recv()
        kept = sums(h, 0, 0, t)
        kept[...] = (kept[...].astype(f32) + land_a[h, t].astype(f32)).astype(bf16)

        @pl.when((s != z) & outer)
        def _():
            onward(h, 0, 0, s, m, kept).start()

    def summed(h, k, p, slot, m):
        if k == 0:
            return sum_a.at[h, slot, m], ra_sem.at[h, slot, m]
        return sum_b.at[h, p, slot, m], rb_sem.at[h, p, slot, m]

    def landing(h, k, p, slot, m):
        ref, recv = summed(h, k, p, slot, m)
        remote(ref, ref, fs_sem.at[h, m], recv, near(h)).wait_recv()
        return ref

    def reduce(k, p, t, s, m):
        for h in range(2):
            ref = landing(h, k, p, s, m)
            ref[...] = (
                ref[...].astype(f32) + sums(h, k, p, t)[...].astype(f32)
            ).astype(bf16)
            onward(h, k, p, s, m, ref).start()

    def gather(h, k, p, t, m):
        first = jnp.where(z == depth - 1, depth, z)
        total = sums(h, k, p, t)[...].astype(f32) + landing(h, k, p, first, m)[...].astype(f32)
        ref, recv = summed(h, k, p, depth, m)

        @pl.when(inner)
        def _():
            landing(h, k, p, depth, m)

        return total + jnp.where(inner, ref[...].astype(f32), 0.0)

    def final(t, m):
        for h in range(2):
            sums(h, 1, 1, t)[...] = gather(h, 1, 1, t, m).astype(bf16)
            final_copy(h, m).start()

    def finish(t, m):
        span = pl.ds(m * rows_mb, rows_mb)
        for h in range(2):
            outs[h][span, 0:cut] = gather(h, 0, 0, t, m).astype(bf16).reshape(rows_mb, cut)
            total = gather(h, 1, 0, t, m)
            final_copy(h, m).wait_recv()
            outs[h][span, cut:width] = (
                (total + land_b[h, m].astype(f32)).astype(bf16).reshape(rows_mb, rest)
            )

    words = plan_words(depth, parts)
    held = [
        sum(jnp.where(z == k, words[k][b], 0) for k in range(depth))
        for b in range(len(words[0]))
    ]

    def run(code):
        kind = lax.div(code, count)
        t = lax.rem(code, count)
        s = lax.div(t, parts)
        m = lax.rem(t, parts)

        def on(low, high=None):
            return pl.when(kind == low if high is None else (kind >= low) & (kind <= high))

        @on(ARRIVE, ARRIVE + 2)
        def _():
            for n, (k, p) in enumerate(PIECES):
                on(ARRIVE + n)(lambda k=k, p=p: arrive(k, p, s, m))

        for h in range(2):
            on(SELECT + h)(lambda h=h: select(h, t, s, m))
        on(EXPERT)(lambda: expert(t))

        @on(COMBINE, PAIR_SUM + 1)
        def _():
            for h in range(2):
                on(COMBINE + h)(lambda h=h: combine(h, t, s, m))
                on(PAIR_SUM + h)(lambda h=h: pair_sum(h, t, s, m))

        @on(REDUCE, REDUCE + 2)
        def _():
            for n, (k, p) in enumerate(PIECES):
                on(REDUCE + n)(lambda k=k, p=p: reduce(k, p, t, s, m))

        @on(OWN, FINISH)
        def _():
            for n, (k, p) in enumerate(PIECES):
                on(OWN + n)(lambda k=k, p=p: spread_own(k, p, m))
            on(PASS_OWN)(lambda: pass_own(0, m))
            on(FINAL)(lambda: final(t, m))
            on(FINISH)(lambda: finish(t, m))

    def block(b, carry):
        word = sum(jnp.where(b == k, held[k], 0) for k in range(len(held)))

        def one(n, word):
            run(lax.rem(word, KINDS * count))
            return lax.div(word, KINDS * count)

        lax.fori_loop(0, PACKED, one, word)
        return carry

    lax.fori_loop(0, len(held), block, 0)

    def drain(t, carry):
        s = lax.div(t, parts)
        m = lax.rem(t, parts)
        for h in range(2):
            spread_p(h, 0, s, m).wait_send()
            pair_copy(h, t).wait_send()
            for q in range(1, 4):
                back_copy(h, t, q).wait_send()

            @pl.when(s == z)
            def _(h=h):
                spread_p(h, 1, s, m).wait_send()
                for k, p in PIECES:

                    @pl.when(z < depth - 1)
                    def _(k=k, p=p):
                        spread_z(h, k, p, z, m, 1).wait_send()

                    @pl.when(z > 0)
                    def _(k=k, p=p):
                        spread_z(h, k, p, z, m, -1, True).wait_send()

            @pl.when(s != z)
            def _(h=h):
                for k, p in PIECES:
                    onward(h, k, p, s, m, sums(h, k, p, t)).wait_send()

                    @pl.when(inner)
                    def _(k=k, p=p):
                        spread_z(h, k, p, s, m, -away(s)).wait_send()

        return carry

    lax.fori_loop(0, count, drain, 0)
    for m in range(parts):
        for h in range(2):
            final_copy(h, m).wait_send()


def settle_kernel(out_ref, grad_ref, out_to, grad_to):
    out_to[...] = out_ref[...]
    grad_to[...] = grad_ref[...]


def settle(out, grad):
    rows, width = out.shape
    spec = pl.BlockSpec((rows // SETTLE, width), lambda i: (i, 0))
    shape = jax.ShapeDtypeStruct(out.shape, out.dtype)
    return pl.pallas_call(
        settle_kernel,
        grid=(SETTLE,),
        out_shape=(shape, shape),
        in_specs=[spec, spec],
        out_specs=(spec, spec),
    )(out, grad)


def plane_cut(width):
    blocks = width // LANES
    return max(1, blocks * 5 // 9) * LANES


def plane_local(
    tokens, cotangent, expert_ids, combine_weights, live_counts, gate_weight, up_weight, down_weight
):
    groups = lax.axis_size("grp")
    peers = lax.axis_size("dev")
    experts = groups * peers
    depth = groups // 2
    rows, width = tokens.shape
    hidden = gate_weight.shape[2]
    parts = live_counts.shape[1]
    rows_mb = rows // parts
    per = rows_mb * expert_ids.shape[1] // experts
    cut = plane_cut(width)
    blocks = rows_mb // per
    rest = width - cut
    count = depth * parts
    slots = 8 * per
    vmem = pl.BlockSpec(memory_space=pltpu.VMEM)
    anywhere = pl.BlockSpec(memory_space=pl.ANY)
    dma = pltpu.SemaphoreType.DMA
    bf16 = jnp.bfloat16
    mixed = pl.pallas_call(
        functools.partial(plane_kernel, groups, parts, experts, per, cut),
        out_shape=(
            jax.ShapeDtypeStruct((rows, width), bf16),
            jax.ShapeDtypeStruct((rows, width), bf16),
        ),
        in_specs=[anywhere] * 2 + [vmem] * 3 + [anywhere] * 3,
        out_specs=(vmem, vmem),
        scratch_shapes=[
            pltpu.VMEM((width, hidden), bf16),
            pltpu.VMEM((width, hidden), bf16),
            pltpu.VMEM((hidden, width), bf16),
            pltpu.VMEM((2, 2, depth, parts, rows_mb, cut + LANES), bf16),
            pltpu.VMEM((2, 2, depth, parts, rows_mb, rest), bf16),
            pltpu.VMEM((2, 2, LANES, slots), bf16),
            pltpu.VMEM((2 * rows_mb, slots), jnp.float32),
            pltpu.VMEM((2, count, 2 * rows_mb, slots), bf16),
            pltpu.VMEM((2, count, 8, per, width), bf16),
            pltpu.VMEM((count, 2, 2, 2, per, width), bf16),
            pltpu.VMEM((count, 2, 2, 2, per, width), bf16),
            pltpu.VMEM((2, count, 4, 2, per, width), bf16),
            pltpu.VMEM((2, count, blocks, per, cut), bf16),
            pltpu.VMEM((2, parts, blocks, per, rest), bf16),
            pltpu.VMEM((2, depth + 1, parts, blocks, per, cut), bf16),
            pltpu.VMEM((2, 2, depth + 1, parts, blocks, per, rest), bf16),
            dma((3,)),
            dma((4, parts)),
            dma((4, 2, depth, parts)),
            dma((4, 2, depth, parts)),
            dma((4, 2, parts)),
            dma((4, depth, parts)),
            dma((2, count, 4)),
            dma((2, count, 4)),
            dma((2, count, 4)),
            dma((2, count, 4)),
            dma((2, count)),
            dma((2, count)),
            dma((2, depth + 1, parts)),
            dma((2, 2, depth + 1, parts)),
            dma((2, 3, depth, parts)),
            dma((2, parts)),
            dma((2, parts)),
        ],
        compiler_params=pltpu.CompilerParams(
            collective_id=0, has_side_effects=True, vmem_limit_bytes=65 * 1024 * 1000
        ),
    )(
        tokens,
        cotangent,
        expert_ids.T,
        combine_weights.T,
        live_counts,
        gate_weight[0],
        up_weight[0],
        down_weight[0],
    )
    return settle(*mixed)


def local(*args):
    groups = lax.axis_size("grp")
    peers = lax.axis_size("dev")
    depth = groups // 2
    fits = 2 * groups * peers <= LANES
    planned = depth in PLANS and args[4].shape[1] == PLAN_PARTS
    if peers == 4 and groups % 2 == 0 and planned and fits:
        return plane_local(*args)
    return general_local(*args)


def solution(mesh):
    spec2 = P(("grp", "dev"), None)
    spec3 = P(("grp", "dev"), None, None)
    return jax.shard_map(
        local,
        mesh=mesh,
        in_specs=(spec2,) * 5 + (spec3,) * 3,
        out_specs=(spec2, spec2),
        check_vma=False,
    )
```

```python
import functools

import jax
import jax.numpy as jnp
from jax import lax
from jax.experimental import pallas as pl
from jax.experimental.pallas import tpu as pltpu
from jax.sharding import PartitionSpec as P

PAIR = 2
LAG_EXPERT = 1
LAG_RETURN = 2
MESH = pl.DeviceIdType.MESH
TRANS_RHS = (((1,), (1,)), ((), ()))


def xor(a, b, size):
    out = 0
    bit = 1
    while bit < size:
        out = out + ((a // bit + b // bit) % 2) * bit
        bit *= 2
    return out


def chunk_order(groups):
    if groups < 8:
        return list(range(groups))
    return [0, 4, 2] + list(range(5, groups)) + [3, 1]


def distance_of(unit, parts, groups):
    i = unit // parts
    out = 0
    for k, value in enumerate(chunk_order(groups)):
        out = out + value * ((i + groups - k) // groups - (i + groups - k - 1) // groups)
    return out


def moe_kernel(
    groups,
    peers,
    joined,
    parts,
    tok_ref,
    cot_ref,
    pick_ref,
    slot_ref,
    sum_ref,
    gate_hbm,
    up_hbm,
    down_hbm,
    out_ref,
    grad_ref,
    gate_ref,
    up_ref,
    down_ref,
    zsend,
    zrecv,
    zback,
    xysend,
    xyrecv,
    xyback,
    w_sem,
    zs_sem,
    zr_sem,
    bs_sem,
    br_sem,
    ds_sem,
    dr_sem,
    rs_sem,
    rr_sem,
):
    g = lax.axis_index("grp")
    l = lax.axis_index("dev")
    width = tok_ref.shape[1]
    wide = 2 * width
    units = groups * parts
    chunks = units // joined
    group_rows = zrecv.shape[1]
    slots = slot_ref.shape[2]
    peer_rows = slots // peers

    barrier = pltpu.get_barrier_semaphore()
    for k in range(1, groups):
        pl.semaphore_signal(
            barrier, inc=1, device_id={"grp": xor(g, k, groups)}, device_id_type=MESH
        )
    for q in range(1, peers):
        pl.semaphore_signal(
            barrier, inc=1, device_id={"dev": xor(l, q, peers)}, device_id_type=MESH
        )

    loads = [
        pltpu.make_async_copy(src, dst, w_sem.at[n])
        for n, (src, dst) in enumerate(
            ((gate_hbm, gate_ref), (up_hbm, up_ref), (down_hbm, down_ref))
        )
    ]
    for load in loads:
        load.start()

    def z_copy(i):
        return pltpu.make_async_remote_copy(
            src_ref=zsend.at[i],
            dst_ref=zrecv.at[i],
            send_sem=zs_sem.at[i],
            recv_sem=zr_sem.at[i],
            device_id={"grp": xor(g, distance_of(i, parts, groups), groups)},
            device_id_type=MESH,
        )

    def z_back(i):
        return pltpu.make_async_remote_copy(
            src_ref=zrecv.at[i, :, pl.ds(0, wide)],
            dst_ref=zback.at[i],
            send_sem=bs_sem.at[i],
            recv_sem=br_sem.at[i],
            device_id={"grp": xor(g, distance_of(i, parts, groups), groups)},
            device_id_type=MESH,
        )

    def xy_copy(c, q):
        return pltpu.make_async_remote_copy(
            src_ref=xysend.at[c, q],
            dst_ref=xyrecv.at[c, q],
            send_sem=ds_sem.at[c, q],
            recv_sem=dr_sem.at[c, q],
            device_id={"dev": xor(l, q, peers)},
            device_id_type=MESH,
        )

    def xy_back(c, q):
        return pltpu.make_async_remote_copy(
            src_ref=xyrecv.at[c, q],
            dst_ref=xyback.at[c, q],
            send_sem=rs_sem.at[c, q],
            recv_sem=rr_sem.at[c, q],
            device_id={"dev": xor(l, q, peers)},
            device_id_type=MESH,
        )

    def fill(i, target):
        pick = pick_ref[i]
        for source, low in ((tok_ref, 0), (cot_ref, width)):
            target[i, :, low : low + width] = jnp.dot(
                pick, source[...], preferred_element_type=jnp.float32
            ).astype(jnp.bfloat16)
        target[i, :, wide : wide + slots] = jnp.dot(
            pick, slot_ref[i // parts], preferred_element_type=jnp.float32
        ).astype(jnp.bfloat16)

    for i in range(parts):
        fill(i, zrecv)

    def chunk_weights(c):
        block = zrecv[pl.ds(c * joined, joined), :, wide : wide + slots]
        return block.reshape(joined * group_rows, slots)

    def place(c):
        for j in range(joined):
            i = c * joined + j

            @pl.when(i >= parts)
            def _(i=i):
                z_copy(i).wait_recv()

        weights = chunk_weights(c).astype(jnp.float32)
        select = jnp.where(weights != 0.0, 1.0, 0.0).T.astype(jnp.bfloat16)
        rows = zrecv[pl.ds(c * joined, joined), :, 0:wide].reshape(joined * group_rows, wide)
        placed = jnp.dot(select, rows, preferred_element_type=jnp.float32).astype(jnp.bfloat16)
        for q in range(1, peers):
            xysend[c, q] = placed[q * peer_rows : (q + 1) * peer_rows]
            xy_copy(c, q).start()
        xyrecv[c, 0] = placed[0:peer_rows]

    def expert(c):
        @pl.when(c == 0)
        def _():
            for load in loads:
                load.wait()

        for q in range(1, peers):
            xy_copy(c, q).wait_recv()
        rows_x = xyrecv[c, :, :, 0:width].reshape(slots, width)
        rows_dy = xyrecv[c, :, :, width:wide].reshape(slots, width)
        gate_pre = jnp.dot(rows_x, gate_ref[...], preferred_element_type=jnp.float32)
        up_pre = jnp.dot(rows_x, up_ref[...], preferred_element_type=jnp.float32)
        act_grad = lax.dot_general(
            rows_dy, down_ref[...], TRANS_RHS, preferred_element_type=jnp.float32
        )
        sig = jax.nn.sigmoid(gate_pre)
        gate_act = gate_pre * sig
        act = (gate_act * up_pre).astype(jnp.bfloat16)
        gate_grad = (act_grad * up_pre * sig * (1.0 + gate_pre * (1.0 - sig))).astype(jnp.bfloat16)
        up_grad = (act_grad * gate_act).astype(jnp.bfloat16)
        expert_out = jnp.dot(act, down_ref[...], preferred_element_type=jnp.float32)
        xyrecv[c, :, :, 0:width] = expert_out.astype(jnp.bfloat16).reshape(peers, peer_rows, width)
        expert_grad = lax.dot_general(
            gate_grad, gate_ref[...], TRANS_RHS, preferred_element_type=jnp.float32
        ) + lax.dot_general(up_grad, up_ref[...], TRANS_RHS, preferred_element_type=jnp.float32)
        xyrecv[c, :, :, width:wide] = expert_grad.astype(jnp.bfloat16).reshape(
            peers, peer_rows, width
        )
        for q in range(1, peers):
            xy_back(c, q).start()
        xyback[c, 0] = xyrecv[c, 0]

    def combine(c):
        for q in range(1, peers):
            xy_back(c, q).wait_recv()
        weights = chunk_weights(c)
        pairs = jnp.dot(
            weights, xyback[c].reshape(slots, wide), preferred_element_type=jnp.float32
        ).astype(jnp.bfloat16)
        zrecv[pl.ds(c * joined, joined), :, 0:wide] = pairs.reshape(joined, group_rows, wide)
        for j in range(joined):
            i = c * joined + j

            @pl.when(i >= parts)
            def _():
                z_back(i).start()

    early = min(1, parts // joined)
    pl.semaphore_wait(barrier, groups + peers - 2)
    for c in range(early):
        place(c)
    fill(parts, zsend)

    def send_step(i, carry):
        fill(i, zsend)
        z_copy(i - 1).start()
        return carry

    lax.fori_loop(parts + 1, units, send_step, 0)
    z_copy(units - 1).start()

    def step(t, carry):
        @pl.when((t >= early) & (t < chunks))
        def _():
            place(t)

        @pl.when((t >= LAG_EXPERT) & (t < chunks + LAG_EXPERT))
        def _():
            expert(t - LAG_EXPERT)

        @pl.when(t >= LAG_RETURN)
        def _():
            combine(t - LAG_RETURN)

        return carry

    lax.fori_loop(0, chunks + LAG_RETURN, step, 0)

    for i in range(parts):
        zback[i] = zrecv[i, :, 0:wide]

    def finish_step(i, carry):
        z_back(i).wait_recv()
        return carry

    lax.fori_loop(parts, units, finish_step, 0)
    for target, low in ((out_ref, 0), (grad_ref, width)):
        target[...] = jnp.dot(
            sum_ref[...],
            zback[:, :, low : low + width].reshape(units * group_rows, width),
            preferred_element_type=jnp.float32,
        ).astype(jnp.bfloat16)

    def drain_z(i, carry):
        z_copy(i).wait_send()
        z_back(i).wait_send()
        return carry

    lax.fori_loop(parts, units, drain_z, 0)

    def drain_xy(c, carry):
        for q in range(1, peers):
            xy_copy(c, q).wait_send()
            xy_back(c, q).wait_send()
        return carry

    lax.fori_loop(0, chunks, drain_xy, 0)


def routing(expert_ids, combine_weights, live_counts, groups, peers, joined):
    rows, top_count = expert_ids.shape
    parts = live_counts.shape[1]
    rows_mb = rows // parts
    experts = groups * peers
    units = groups * parts
    per_expert = rows_mb * top_count // experts
    per_group = per_expert * peers // PAIR
    g = lax.axis_index("grp")
    l = lax.axis_index("dev")
    relative = ((expert_ids // peers) ^ g) * peers + ((expert_ids % peers) ^ l)
    order = jnp.array(chunk_order(groups), jnp.int32)
    wanted = (order[:, None] * peers + jnp.arange(peers, dtype=jnp.int32)).reshape(-1)
    hit = relative[:, :, None] == wanted
    member = jnp.any(hit, axis=1)
    weight = jnp.sum(
        jnp.where(hit, combine_weights.astype(jnp.float32)[:, :, None], 0.0), axis=1
    )
    index = jnp.arange(rows, dtype=jnp.int32)
    part = index // rows_mb
    live = (index % rows_mb) < jnp.repeat(live_counts[0], rows_mb)
    weight = jnp.where(live[:, None], weight, 0.0).astype(jnp.bfloat16)
    in_group = jnp.any(member.reshape(rows, groups, peers), axis=2)
    both = jnp.concatenate([member, in_group], axis=1).astype(jnp.bfloat16)
    before = (
        (index[:, None] > index[None, :]) & (part[:, None] == part[None, :])
    ).astype(jnp.bfloat16)
    rank = jnp.dot(before, both, preferred_element_type=jnp.float32).astype(jnp.int32)
    expert_rank, group_rank = rank[:, :experts], rank[:, experts:]
    group_slot = jnp.where(in_group, group_rank + part[:, None] * per_group, -1)
    unit_rows = jnp.arange(parts * per_group, dtype=jnp.int32)
    pick = (
        (group_slot.T[:, None, :] == unit_rows[None, :, None])
        .astype(jnp.bfloat16)
        .reshape(units, per_group, rows)
    )
    total = (
        (group_slot[:, :, None] == unit_rows)
        .astype(jnp.bfloat16)
        .reshape(rows, units * per_group)
    )
    width = joined * per_expert
    offset = jnp.arange(groups, dtype=jnp.int32)[None, :] * parts + part[:, None]
    expert_slot = expert_rank.reshape(rows, groups, peers) + (
        offset % joined * per_expert
    )[..., None]
    expert_slot = expert_slot.transpose(1, 0, 2)[..., None]
    slot = jnp.where(
        expert_slot == jnp.arange(width, dtype=jnp.int32),
        weight.reshape(rows, groups, peers).transpose(1, 0, 2)[..., None],
        jnp.zeros((), jnp.bfloat16),
    ).reshape(groups, rows, peers * width)
    return pick, slot, total


def general_local(
    tokens, cotangent, expert_ids, combine_weights, live_counts, gate_weight, up_weight, down_weight
):
    groups = lax.axis_size("grp")
    peers = lax.axis_size("dev")
    rows, width = tokens.shape
    hidden = gate_weight.shape[2]
    parts = live_counts.shape[1]
    units = groups * parts
    per_expert = rows // parts * expert_ids.shape[1] // (groups * peers)
    per_group = per_expert * peers // PAIR
    joined = max(1, 16 // per_expert)
    chunks = units // joined
    peer_rows = joined * per_expert
    slots = peers * peer_rows
    wide = 2 * width
    pick, slot, total = routing(
        expert_ids, combine_weights, live_counts, groups, peers, joined
    )
    vmem = pl.BlockSpec(memory_space=pltpu.VMEM)
    anywhere = pl.BlockSpec(memory_space=pl.ANY)
    dma = pltpu.SemaphoreType.DMA
    bf16 = jnp.bfloat16
    return pl.pallas_call(
        functools.partial(moe_kernel, groups, peers, joined, parts),
        out_shape=(
            jax.ShapeDtypeStruct((rows, width), bf16),
            jax.ShapeDtypeStruct((rows, width), bf16),
        ),
        in_specs=[vmem] * 5 + [anywhere] * 3,
        out_specs=(vmem, vmem),
        scratch_shapes=[
            pltpu.VMEM((width, hidden), bf16),
            pltpu.VMEM((width, hidden), bf16),
            pltpu.VMEM((hidden, width), bf16),
            pltpu.VMEM((units, per_group, wide + slots), bf16),
            pltpu.VMEM((units, per_group, wide + slots), bf16),
            pltpu.VMEM((units, per_group, wide), bf16),
            pltpu.VMEM((chunks, peers, peer_rows, wide), bf16),
            pltpu.VMEM((chunks, peers, peer_rows, wide), bf16),
            pltpu.VMEM((chunks, peers, peer_rows, wide), bf16),
            dma((3,)),
            dma((units,)),
            dma((units,)),
            dma((units,)),
            dma((units,)),
            dma((chunks, peers)),
            dma((chunks, peers)),
            dma((chunks, peers)),
            dma((chunks, peers)),
        ],
        compiler_params=pltpu.CompilerParams(
            collective_id=0, has_side_effects=True, vmem_limit_bytes=65 * 1024 * 1000
        ),
    )(
        tokens,
        cotangent,
        pick,
        slot,
        total,
        gate_weight[0],
        up_weight[0],
        down_weight[0],
    )


LANES = 128
SETTLE = 2
SPREAD_SHARE = 10
SUM_SHARE = 9


PIECES = ((0, 0), (1, 0), (1, 1))
ARRIVE, SELECT, EXPERT, COMBINE, PAIR_SUM, REDUCE = 0, 3, 5, 6, 8, 10
OWN, PASS_OWN, FINAL, FINISH, IDLE = 13, 16, 17, 18, 19
KINDS = 32
PACKED = 3
PLAN_PARTS = 2
PLAN_4 = (
    (
        120, 24, 32, 105, 2, 121, 129, 18, 10, 34, 113, 26, 4, 33, 25, 20, 42, 12, 36, 28, 6,
        58, 50, 44, 22, 14, 66, 30, 38, 52, 7, 15, 60, 46, 74, 68, 76, 23, 39, 31, 11, 62, 13,
        41, 47, 54, 5, 19, 63, 55, 21, 37, 29, 3, 79, 71, 45, 70, 35, 27, 49, 78, 61, 53, 43,
        77, 40, 65, 69, 57, 51, 59, 48, 137, 67, 73, 75, 56, 136, 64, 72, 144, 145,
    ),
    (
        122, 34, 26, 4, 0, 16, 20, 12, 8, 28, 36, 1, 24, 32, 6, 22, 14, 9, 44, 7, 40, 15, 30,
        17, 38, 52, 115, 60, 131, 48, 23, 39, 13, 107, 31, 123, 46, 25, 27, 33, 100, 92, 62,
        76, 64, 5, 68, 84, 21, 47, 29, 35, 54, 42, 63, 56, 37, 102, 55, 41, 94, 95, 103, 96,
        88, 45, 78, 70, 79, 43, 86, 71, 57, 87, 61, 49, 53, 89, 97, 101, 50, 65, 51, 58, 72,
        80, 77, 93, 138, 69, 73, 85, 59, 66, 74, 81, 75, 139, 67, 146, 147,
    ),
)
PLANS = {4: PLAN_4}


def plan_words(depth, parts):
    count = depth * parts
    base = KINDS * count
    orders = []
    for z in range(depth):
        codes = list(PLANS[depth][min(z, depth - 1 - z)])
        if 2 * z >= depth:
            codes = [
                kind - kind % count + (depth - 1 - kind % count // parts) * parts + kind % parts
                for kind in codes
            ]
        if codes.pop() != FINISH * count + (z + 1) * parts - 1:
            raise ValueError("plan")
        orders.append(codes)
    length = max(len(codes) for codes in orders)
    length += -length % PACKED
    words = []
    for codes in orders:
        codes = codes + [IDLE * count] * (length - len(codes))
        words.append(
            [
                sum(codes[b + n] * base**n for n in range(PACKED))
                for b in range(0, length, PACKED)
            ]
        )
    return words


def plane_kernel(
    groups,
    parts,
    experts,
    per,
    cut,
    back,
    tok_hbm,
    cot_hbm,
    ids_ref,
    mix_ref,
    live_ref,
    gate_hbm,
    up_hbm,
    down_hbm,
    out_ref,
    grad_ref,
    gate_ref,
    up_ref,
    down_ref,
    dense_a,
    dense_b,
    hot_ref,
    slot_ref,
    weight_ref,
    send_ref,
    moved_x,
    moved_dy,
    back_ref,
    land_a,
    land_b,
    sum_a,
    sum_b,
    w_sem,
    in_sem,
    agr_sem,
    agz_sem,
    agd_sem,
    agp_sem,
    ss_sem,
    sr_sem,
    bs_sem,
    br_sem,
    ps_sem,
    pr_sem,
    ra_sem,
    rb_sem,
    rs_sem,
    fs_sem,
    fr_sem,
):
    g = lax.axis_index("grp")
    l = lax.axis_index("dev")
    depth = groups // 2
    z = g // 2
    core = g % 2
    peers = experts // groups
    rows_mb = dense_a.shape[4]
    rows = rows_mb * parts
    width = down_ref.shape[1]
    count = depth * parts
    pair = 2 * per
    blocks = rows_mb // per
    slots = 4 * pair
    both = 2 * rows_mb
    f32 = jnp.float32
    bf16 = jnp.bfloat16
    inner = (z > 0) & (z < depth - 1)
    outer = (z == 0) | (z == depth - 1)
    dense = (dense_a, dense_b)
    size = (cut, width - cut)
    sum_size = (back, width - back)
    outs = (out_ref, grad_ref)

    flips = (l + 2 - 4 * (l // 2), l + 1 - 2 * (l % 2))

    def near(h):
        return {"grp": g, "dev": flips[1 - h]}

    def peer(h, q):
        return {
            "grp": g + (q // 2) * (1 - 2 * core),
            "dev": flips[h] if q % 2 else l,
        }

    def remote(src, dst, send, recv, device):
        return pltpu.make_async_remote_copy(
            src_ref=src,
            dst_ref=dst,
            send_sem=send,
            recv_sem=recv,
            device_id=device,
            device_id_type=MESH,
        )

    def block(h, k, p, s, m, tables):
        extra = LANES if k == 0 and tables else 0
        return dense[k].at[h, p, s, m, :, pl.ds(0, size[k] + extra)]

    def by_part(k, m, fn):
        if k == 1:
            fn(False)
        elif isinstance(m, int):
            fn(m == 0)
        else:
            pl.when(m == 0)(lambda: fn(True))
            pl.when(m != 0)(lambda: fn(False))

    def spread_z(h, k, p, s, m, d, first, second=False):
        slot = block(h, k, p, s, m, first and h == 0)
        send = agd_sem.at[2 * h + k, p, m] if second else agz_sem.at[2 * h + k, p, s, m]
        return remote(
            slot, slot, send, agr_sem.at[2 * h + k, p, s, m], {"grp": g + 2 * d, "dev": l}
        )

    def spread_p(h, k, s, m, first):
        return remote(
            block(h, k, 0, s, m, first),
            block(h, k, 1, s, m, first),
            agp_sem.at[2 * h + k, s, m],
            agr_sem.at[2 * h + k, 1, s, m],
            near(h),
        )

    def moved(h, t, q):
        if h == 0:
            return moved_x.at[t, q // 2, q % 2]
        return moved_dy.at[t, q // 2, :, q % 2]

    def select_copy(h, t, q):
        return remote(
            send_ref.at[h, t, pl.ds(2 * q, 2)],
            moved(h, t, q),
            ss_sem.at[h, t, q],
            sr_sem.at[h, t, q],
            peer(h, q),
        )

    def back_copy(h, t, q):
        return remote(
            moved(h, t, q),
            back_ref.at[h, t, q],
            bs_sem.at[h, t, q],
            br_sem.at[h, t, q],
            peer(h, q),
        )

    def sums(h, k, p, t):
        low = 0 if k == 0 else back
        return send_ref.at[h, t, pl.ds(p * blocks, blocks), :, pl.ds(low, sum_size[k])]

    def pair_copy(h, t):
        return remote(
            sums(h, 0, 1, t), land_a.at[h, t], ps_sem.at[h, t], pr_sem.at[h, t], near(h)
        )

    def away(s):
        return jnp.where(s > z, 1, -1)

    def onward(h, k, p, s, m, src):
        slot = jnp.where(s == z + 1, depth, s)
        if k == 0:
            dst, recv = sum_a.at[h, slot, m], ra_sem.at[h, slot, m]
        else:
            dst, recv = sum_b.at[h, p, slot, m], rb_sem.at[h, p, slot, m]
        return remote(
            src, dst, rs_sem.at[h, k + p, s, m], recv, {"grp": g + 2 * away(s), "dev": l}
        )

    def final_copy(h, m):
        return remote(
            sums(h, 1, 1, z * parts + m),
            land_b.at[h, m],
            fs_sem.at[h, m],
            fr_sem.at[h, m],
            near(h),
        )

    barrier = pltpu.get_barrier_semaphore()

    def greet(device):
        pl.semaphore_signal(barrier, inc=1, device_id=device, device_id_type=MESH)

    @pl.when(z > 0)
    def _():
        greet({"grp": g - 2, "dev": l})

    @pl.when(z < depth - 1)
    def _():
        greet({"grp": g + 2, "dev": l})

    greet(peer(0, 2))
    for h in range(2):
        greet(peer(h, 1))
        greet(peer(h, 3))

    ins = []
    for h, src in ((0, tok_hbm), (1, cot_hbm)):
        for m in range(parts):
            for k, low in ((1, cut), (0, 0)):
                copy = pltpu.make_async_copy(
                    src.at[pl.ds(m * rows_mb, rows_mb), pl.ds(low, size[k])],
                    dense[k].at[h, 0, z, m, :, pl.ds(0, size[k])],
                    in_sem.at[2 * h + k, m],
                )
                copy.start()
                ins.append((k, copy))
    loads = [
        pltpu.make_async_copy(src, dst, w_sem.at[n])
        for n, (src, dst) in enumerate(
            ((gate_hbm, gate_ref), (up_hbm, up_ref), (down_hbm, down_ref))
        )
    ]
    for load in loads:
        load.start()

    def send_own(h, k, p, m, first):
        @pl.when(z < depth - 1)
        def _():
            spread_z(h, k, p, z, m, 1, first).start()

        @pl.when(z > 0)
        def _():
            spread_z(h, k, p, z, m, -1, first, True).start()

    def spread_own(k, p, m):
        def go(first):
            for h in range(2):
                if p == 1:
                    spread_p(h, 1, z, m, first).wait_recv()
                send_own(h, k, p, m, first)

        by_part(k, m, go)

    def pass_own(k, m):
        def go(first):
            for h in range(2):
                spread_p(h, k, z, m, first).start()

        by_part(k, m, go)

    pl.semaphore_wait(barrier, 5 + jnp.where(inner, 2, 1))
    for k, copy in ins:
        if k == 1:
            copy.wait()
    pass_own(1, 0)
    spread_own(1, 0, 0)

    lane = lax.broadcasted_iota(jnp.int32, (LANES, rows), 0)
    row = lax.broadcasted_iota(jnp.int32, (LANES, rows), 1)
    shift = 2 * experts * lax.div(row, rows_mb)
    ids = ids_ref[...]
    mix = mix_ref[...].astype(f32)
    weight = jnp.zeros((LANES, rows), f32)
    named = jnp.zeros((LANES, rows), f32)
    for k in range(ids.shape[0]):
        expert_id = ids[k : k + 1] + shift
        weight = weight + jnp.where(lane == expert_id, mix[k : k + 1], 0.0)
        named = named + jnp.where(lane == expert_id + experts, 1.0, 0.0)
    lives = live_ref[...]
    alive = jnp.zeros((LANES, rows), f32)
    for m in range(parts):
        first = m * rows_mb
        alive = alive + jnp.where(
            (row >= first) & (row < first + lives[0:1, m : m + 1]), 1.0, 0.0
        )
    row_a = lax.broadcasted_iota(jnp.int32, (rows, rows), 1)
    row_b = lax.broadcasted_iota(jnp.int32, (rows, rows), 0)
    before = jnp.where(
        (row_a > row_b) & (lax.div(row_a, rows_mb) == lax.div(row_b, rows_mb)), 1.0, 0.0
    ).astype(bf16)
    rank = jnp.dot(named.astype(bf16), before, preferred_element_type=f32)
    routes = (weight * alive + rank).T
    packed = routes[0:rows_mb]
    for m in range(1, parts):
        packed = packed + routes[m * rows_mb : (m + 1) * rows_mb]
    packed = packed.astype(bf16)
    for h in range(2):
        dense_a[h, 0, z, 0, :, cut : cut + LANES] = packed
    for k, copy in ins:
        if k == 0:
            copy.wait()
    spread_own(0, 0, 0)
    pass_own(0, 0)
    for m in range(1, parts):
        pass_own(1, m)

    lane_k = lax.broadcasted_iota(jnp.int32, (LANES, slots), 0)
    slot_k = lax.broadcasted_iota(jnp.int32, (LANES, slots), 1)
    quad = lax.div(slot_k, pair)
    owner = 2 * z + core + lax.div(quad, 2) * (1 - 2 * core)
    for h in range(2):
        target = owner * peers + jnp.where(lax.rem(quad, 2) == 1, flips[h], l)
        for m in range(parts):
            for n in range(2):
                hot_ref[h, m, n] = jnp.where(
                    lane_k == target + (2 * m + n) * experts, 1.0, 0.0
                ).astype(bf16)
    row_s = lax.broadcasted_iota(jnp.int32, (both, slots), 0)
    col_s = lax.broadcasted_iota(jnp.int32, (both, slots), 1)
    slot_ref[...] = jnp.where(
        lax.div(row_s, rows_mb) == lax.rem(lax.div(col_s, per), 2), lax.rem(col_s, per), -1
    ).astype(f32)

    for load in loads:
        load.wait()

    def arrive(k, p, s, m):
        def go(first):
            for h in range(2):
                copy = spread_z(h, k, p, s, m, -away(s), first)
                copy.wait_recv()
                if k == 0:
                    if h == 1 and first:
                        dense_a[1, 0, s, 0, :, cut : cut + LANES] = dense_a[
                            0, 0, s, 0, :, cut : cut + LANES
                        ]
                    spread_p(h, 0, s, m, first).start()

                @pl.when(inner)
                def _(copy=copy):
                    copy.start()

        by_part(k, m, go)

    def select(h, t, s, m):
        by_part(0, m, lambda first: spread_p(h, 0, s, m, first).wait_recv())
        routes = dense_a[h, :, s, 0, :, cut : cut + LANES].reshape(both, LANES)
        weights = jnp.dot(routes, hot_ref[h, m, 0], preferred_element_type=f32)
        ranks = jnp.dot(routes, hot_ref[h, m, 1], preferred_element_type=f32)
        weights = jnp.where(ranks == slot_ref[...], weights, 0.0)
        weight_ref[h, t] = weights.astype(bf16)
        pick = jnp.where(weights != 0.0, 1.0, 0.0).T.astype(bf16)
        for k, low in ((0, 0), (1, cut)):
            span = slice(low, low + size[k])
            placed = jnp.dot(
                pick,
                dense[k][h, :, s, m, :, 0 : size[k]].reshape(both, size[k]),
                preferred_element_type=f32,
            ).astype(bf16)
            kept = placed[0:pair].reshape(2, per, size[k])
            if h == 0:
                moved_x[t, 0, 0, :, :, span] = kept
            else:
                moved_dy[t, 0, :, 0, :, span] = kept
            send_ref[h, t, 2:8, :, span] = placed[pair:slots].reshape(6, per, size[k])
        for q in range(1, 4):
            select_copy(h, t, q).start()

    def expert(t):
        for h in range(2):
            for q in range(1, 4):
                select_copy(h, t, q).wait_recv()
        rows_x = moved_x[t].reshape(slots, width)
        rows_dy = moved_dy[t].reshape(slots, width)
        gate_pre = jnp.dot(rows_x, gate_ref[...], preferred_element_type=f32)
        up_pre = jnp.dot(rows_x, up_ref[...], preferred_element_type=f32)
        act_grad = lax.dot_general(
            rows_dy, down_ref[...], TRANS_RHS, preferred_element_type=f32
        )
        sig = jax.nn.sigmoid(gate_pre)
        gate_act = gate_pre * sig
        act = (gate_act * up_pre).astype(bf16)
        gate_grad = (act_grad * up_pre * sig * (1.0 + gate_pre * (1.0 - sig))).astype(bf16)
        up_grad = (act_grad * gate_act).astype(bf16)
        expert_out = jnp.dot(act, down_ref[...], preferred_element_type=f32)
        moved_x[t] = expert_out.astype(bf16).reshape(2, 2, 2, per, width)
        for q in range(1, 4):
            back_copy(0, t, q).start()
        expert_grad = lax.dot_general(
            gate_grad, gate_ref[...], TRANS_RHS, preferred_element_type=f32
        ) + lax.dot_general(up_grad, up_ref[...], TRANS_RHS, preferred_element_type=f32)
        moved_dy[t] = expert_grad.astype(bf16).reshape(2, 2, 2, per, width)
        for q in range(1, 4):
            back_copy(1, t, q).start()
        back_ref[0, t, 0] = moved_x[t, 0, 0]
        back_ref[1, t, 0] = moved_dy[t, 0, :, 0]

    def combine(h, t, s, m):
        for q in range(1, 4):
            back_copy(h, t, q).wait_recv()
            select_copy(h, t, q).wait_send()
        send_ref[h, t] = (
            jnp.dot(
                weight_ref[h, t],
                back_ref[h, t].reshape(slots, width),
                preferred_element_type=f32,
            )
            .astype(bf16)
            .reshape(2 * blocks, per, width)
        )
        pair_copy(h, t).start()

        @pl.when((s != z) & outer)
        def _():
            for p in range(2):
                onward(h, 1, p, s, m, sums(h, 1, p, t)).start()

    def pair_sum(h, t, s, m):
        pair_copy(h, t).wait_recv()
        kept = sums(h, 0, 0, t)
        kept[...] = (kept[...].astype(f32) + land_a[h, t].astype(f32)).astype(bf16)

        @pl.when((s != z) & outer)
        def _():
            onward(h, 0, 0, s, m, kept).start()

    def summed(h, k, p, slot, m):
        if k == 0:
            return sum_a.at[h, slot, m], ra_sem.at[h, slot, m]
        return sum_b.at[h, p, slot, m], rb_sem.at[h, p, slot, m]

    def landing(h, k, p, slot, m):
        ref, recv = summed(h, k, p, slot, m)
        remote(ref, ref, fs_sem.at[h, m], recv, near(h)).wait_recv()
        return ref

    def reduce(k, p, t, s, m):
        for h in range(2):
            ref = landing(h, k, p, s, m)
            ref[...] = (
                ref[...].astype(f32) + sums(h, k, p, t)[...].astype(f32)
            ).astype(bf16)
            onward(h, k, p, s, m, ref).start()

    def gather(h, k, p, t, m):
        first = jnp.where(z == depth - 1, depth, z)
        total = sums(h, k, p, t)[...].astype(f32) + landing(h, k, p, first, m)[...].astype(f32)
        ref, recv = summed(h, k, p, depth, m)

        @pl.when(inner)
        def _():
            landing(h, k, p, depth, m)

        return total + jnp.where(inner, ref[...].astype(f32), 0.0)

    def final(t, m):
        for h in range(2):
            sums(h, 1, 1, t)[...] = gather(h, 1, 1, t, m).astype(bf16)
            final_copy(h, m).start()

    def finish(t, m):
        span = pl.ds(m * rows_mb, rows_mb)
        for h in range(2):
            outs[h][span, 0:back] = gather(h, 0, 0, t, m).astype(bf16).reshape(rows_mb, back)
            total = gather(h, 1, 0, t, m)
            final_copy(h, m).wait_recv()
            outs[h][span, back:width] = (
                (total + land_b[h, m].astype(f32)).astype(bf16).reshape(rows_mb, width - back)
            )

    words = plan_words(depth, parts)
    held = [
        sum(jnp.where(z == k, words[k][b], 0) for k in range(depth))
        for b in range(len(words[0]))
    ]

    def run(code):
        kind = lax.div(code, count)
        t = lax.rem(code, count)
        s = lax.div(t, parts)
        m = lax.rem(t, parts)

        def on(low, high=None):
            return pl.when(kind == low if high is None else (kind >= low) & (kind <= high))

        @on(ARRIVE, ARRIVE + 2)
        def _():
            for n, (k, p) in enumerate(PIECES):
                on(ARRIVE + n)(lambda k=k, p=p: arrive(k, p, s, m))

        for h in range(2):
            on(SELECT + h)(lambda h=h: select(h, t, s, m))
        on(EXPERT)(lambda: expert(t))

        @on(COMBINE, PAIR_SUM + 1)
        def _():
            for h in range(2):
                on(COMBINE + h)(lambda h=h: combine(h, t, s, m))
                on(PAIR_SUM + h)(lambda h=h: pair_sum(h, t, s, m))

        @on(REDUCE, REDUCE + 2)
        def _():
            for n, (k, p) in enumerate(PIECES):
                on(REDUCE + n)(lambda k=k, p=p: reduce(k, p, t, s, m))

        @on(OWN, FINISH)
        def _():
            for n, (k, p) in enumerate(PIECES):
                on(OWN + n)(lambda k=k, p=p: spread_own(k, p, m))
            on(PASS_OWN)(lambda: pass_own(0, m))
            on(FINAL)(lambda: final(t, m))
            on(FINISH)(lambda: finish(t, m))

    def batch(b, carry):
        word = sum(jnp.where(b == k, held[k], 0) for k in range(len(held)))

        def one(n, word):
            run(lax.rem(word, KINDS * count))
            return lax.div(word, KINDS * count)

        lax.fori_loop(0, PACKED, one, word)
        return carry

    lax.fori_loop(0, len(held), batch, 0)

    def drain(t, carry):
        s = lax.div(t, parts)
        m = lax.rem(t, parts)
        for h in range(2):
            pair_copy(h, t).wait_send()
            for q in range(1, 4):
                back_copy(h, t, q).wait_send()
        for k, p in PIECES:

            def go(first, k=k, p=p):
                for h in range(2):
                    if p == 0:

                        @pl.when((s == z) | (k == 0))
                        def _(h=h):
                            spread_p(h, k, s, m, first).wait_send()

                    @pl.when((s == z) & (z < depth - 1))
                    def _(h=h):
                        spread_z(h, k, p, z, m, 1, first).wait_send()

                    @pl.when((s == z) & (z > 0))
                    def _(h=h):
                        spread_z(h, k, p, z, m, -1, first, True).wait_send()

                    @pl.when((s != z) & inner)
                    def _(h=h):
                        spread_z(h, k, p, s, m, -away(s), first).wait_send()

            by_part(k, m, go)

            @pl.when(s != z)
            def _(k=k, p=p):
                for h in range(2):
                    onward(h, k, p, s, m, sums(h, k, p, t)).wait_send()

        return carry

    lax.fori_loop(0, count, drain, 0)
    for m in range(parts):
        for h in range(2):
            final_copy(h, m).wait_send()
    finish(z * parts + parts - 1, parts - 1)


def settle_kernel(out_ref, grad_ref, out_to, grad_to):
    out_to[...] = out_ref[...]
    grad_to[...] = grad_ref[...]


def settle(out, grad):
    rows, width = out.shape
    spec = pl.BlockSpec((rows // SETTLE, width), lambda i: (i, 0))
    shape = jax.ShapeDtypeStruct(out.shape, out.dtype)
    return pl.pallas_call(
        settle_kernel,
        grid=(SETTLE,),
        out_shape=(shape, shape),
        in_specs=[spec, spec],
        out_specs=(spec, spec),
    )(out, grad)


def plane_cut(width, share):
    blocks = width // LANES
    return max(1, blocks * share // 18) * LANES


def plane_local(
    tokens, cotangent, expert_ids, combine_weights, live_counts, gate_weight, up_weight, down_weight
):
    groups = lax.axis_size("grp")
    peers = lax.axis_size("dev")
    experts = groups * peers
    depth = groups // 2
    rows, width = tokens.shape
    hidden = gate_weight.shape[2]
    parts = live_counts.shape[1]
    rows_mb = rows // parts
    per = rows_mb * expert_ids.shape[1] // experts
    cut = plane_cut(width, SPREAD_SHARE)
    back = plane_cut(width, SUM_SHARE)
    blocks = rows_mb // per
    rest = width - cut
    count = depth * parts
    slots = 8 * per
    vmem = pl.BlockSpec(memory_space=pltpu.VMEM)
    anywhere = pl.BlockSpec(memory_space=pl.ANY)
    dma = pltpu.SemaphoreType.DMA
    bf16 = jnp.bfloat16
    mixed = pl.pallas_call(
        functools.partial(plane_kernel, groups, parts, experts, per, cut, back),
        out_shape=(
            jax.ShapeDtypeStruct((rows, width), bf16),
            jax.ShapeDtypeStruct((rows, width), bf16),
        ),
        in_specs=[anywhere] * 2 + [vmem] * 3 + [anywhere] * 3,
        out_specs=(vmem, vmem),
        scratch_shapes=[
            pltpu.VMEM((width, hidden), bf16),
            pltpu.VMEM((width, hidden), bf16),
            pltpu.VMEM((hidden, width), bf16),
            pltpu.VMEM((2, 2, depth, parts, rows_mb, cut + LANES), bf16),
            pltpu.VMEM((2, 2, depth, parts, rows_mb, rest), bf16),
            pltpu.VMEM((2, parts, 2, LANES, slots), bf16),
            pltpu.VMEM((2 * rows_mb, slots), jnp.float32),
            pltpu.VMEM((2, count, 2 * rows_mb, slots), bf16),
            pltpu.VMEM((2, count, 8, per, width), bf16),
            pltpu.VMEM((count, 2, 2, 2, per, width), bf16),
            pltpu.VMEM((count, 2, 2, 2, per, width), bf16),
            pltpu.VMEM((2, count, 4, 2, per, width), bf16),
            pltpu.VMEM((2, count, blocks, per, back), bf16),
            pltpu.VMEM((2, parts, blocks, per, width - back), bf16),
            pltpu.VMEM((2, depth + 1, parts, blocks, per, back), bf16),
            pltpu.VMEM((2, 2, depth + 1, parts, blocks, per, width - back), bf16),
            dma((3,)),
            dma((4, parts)),
            dma((4, 2, depth, parts)),
            dma((4, 2, depth, parts)),
            dma((4, 2, parts)),
            dma((4, depth, parts)),
            dma((2, count, 4)),
            dma((2, count, 4)),
            dma((2, count, 4)),
            dma((2, count, 4)),
            dma((2, count)),
            dma((2, count)),
            dma((2, depth + 1, parts)),
            dma((2, 2, depth + 1, parts)),
            dma((2, 3, depth, parts)),
            dma((2, parts)),
            dma((2, parts)),
        ],
        compiler_params=pltpu.CompilerParams(
            collective_id=0, has_side_effects=True, vmem_limit_bytes=65 * 1024 * 1000
        ),
    )(
        tokens,
        cotangent,
        expert_ids.T,
        combine_weights.T,
        live_counts,
        gate_weight[0],
        up_weight[0],
        down_weight[0],
    )
    return settle(*mixed)


def local(*args):
    groups = lax.axis_size("grp")
    peers = lax.axis_size("dev")
    depth = groups // 2
    fits = 2 * PLAN_PARTS * groups * peers <= LANES
    planned = depth in PLANS and args[4].shape[1] == PLAN_PARTS
    if peers == 4 and groups % 2 == 0 and planned and fits:
        return plane_local(*args)
    return general_local(*args)


def solution(mesh):
    spec2 = P(("grp", "dev"), None)
    spec3 = P(("grp", "dev"), None, None)
    return jax.shard_map(
        local,
        mesh=mesh,
        in_specs=(spec2,) * 5 + (spec3,) * 3,
        out_specs=(spec2, spec2),
        check_vma=False,
    )
```
